512 devices in a mesh: wave: 8 (over x, core), plane: 64 (over y, z).
Axes of the slice: x: 4, y: 4, z: 16, core: 2. Of those that a mesh axis runs over, the one named last changes fastest.
Arguments:
- right_side: float32 [8, 512, 128], P('wave', 'plane'), may hold values from -40 to 40
- coupling_x: float32 [512, 128], P('plane'), may hold values from 2 to 6
- coupling_y: float32 [8, 128], P('wave'), may hold values from 0.2 to 0.6
- coupling_z: float32 [8, 512, 128], P('wave', 'plane'), may hold values from 0.3 to 1
- inverse: float32 [8, 512, 128, 128], P('wave', 'plane'), may hold values from -0.05 to 0.15
Outputs:
- solution: float32 [8, 512, 128], P('wave', 'plane')
- residual: float32 [8, 512, 128], P('wave', 'plane')
The draws below stay inside these ranges and needn't reach their ends.
All inputs are finite; a program needn't handle non-finite values.
Results may differ from the reference program's by a relative error of at most 0.0003.
Values sent between devices are 32-bit elements; how exact they have to be, the bound alone decides.
No kernel may reach another device: no remote copies, remote signals or barrier semaphores. Data moves between devices by JAX's collectives and lax.ppermute only.
A program may use at most 64 MiB of HBM per device.

```python
import math
import jax
import jax.numpy as jnp
from jax import lax

B = 128
ITERS = 2
NX = 8
NY = 512


def draw_right_side(key, part):
    first = jax.random.fold_in(jax.random.fold_in(key, 11), 0)
    xs = jnp.arange(NX, dtype=jnp.float32)[:, None, None] / NX
    ys = jnp.arange(NY, dtype=jnp.float32)[None, :, None] / NY
    ramp = jnp.power(3.0, ys) * jnp.power(3.0, xs)
    return jnp.clip(jax.random.normal(first, (NX, NY, B), jnp.float32), -4.0, 4.0) * ramp


def draw_inverse(key, part):
    first, second = jax.random.split(jax.random.fold_in(key, 23))
    diagonal = jax.random.uniform(first, (NX, NY, B), jnp.float32, 0.08, 0.13)
    spread = 0.025
    noise = jax.random.normal(second, (NX, NY, B, B), jnp.float32)
    symmetric = (noise + jnp.swapaxes(noise, -1, -2)) * (spread / (1.4142135 * jnp.sqrt(jnp.float32(B))))
    identity = jnp.eye(B, dtype=jnp.float32)
    return symmetric * (1.0 - identity) + diagonal[..., None] * identity


def block_scale(key, shape, cuts, least, high):
    def one(position, shards_of):
        heights = jax.random.uniform(jax.random.fold_in(jax.random.fold_in(key, 6), position), (shards_of,), jnp.float32, least / len(cuts), high / len(cuts))
        return jnp.repeat(jnp.exp(heights), shape[position] // shards_of).reshape((-1,) + (1,) * (len(shape) - position - 1))

    loudness = one(*cuts[0])
    for cut in cuts[1:]:
        loudness = loudness * one(*cut)
    return loudness


def setup_inputs(seed: int = 0) -> dict:
    key_of = jax.random.split(jax.random.key(seed), 6)
    return {
        "right_side": draw_right_side(jax.random.fold_in(key_of[5], 71), 0),
        "coupling_x": jnp.clip(jnp.exp(math.log(6.0) - 1.0986123 * jax.random.uniform(key_of[1], (NY, B), jnp.float32) ** block_scale(key_of[1], (NY, B), ((0, 64),), -0.2, 0.2)), 2.0, 6.0),
        "coupling_y": jnp.clip(jnp.exp(math.log(0.6) - 1.0986123 * jax.random.uniform(key_of[2], (NX, B), jnp.float32) ** block_scale(key_of[2], (NX, B), ((0, 8),), -0.2, 0.2)), 0.2, 0.6),
        "coupling_z": jnp.clip(jnp.exp(math.log(1.0) - 1.2039728 * jax.random.uniform(key_of[3], (NX, NY, B), jnp.float32) ** block_scale(key_of[3], (NX, NY, B), ((0, 8), (1, 64)), -0.2, 0.2)), 0.3, 1.0),
        "inverse": draw_inverse(jax.random.fold_in(key_of[5], 71), 0),
    }


relax = 1.5


def apply_block(block, vector):
    return jnp.einsum("cij,cj->ci", block, vector, precision=lax.Precision.HIGHEST)


def column_part(values, coupling_x, coupling_y, coupling_z):
    below = jnp.concatenate([jnp.zeros_like(values[..., :1]), values[..., :-1]], axis=-1)
    above = jnp.concatenate([values[..., 1:], jnp.zeros_like(values[..., :1])], axis=-1)
    upper_z = jnp.concatenate([coupling_z[..., 1:], coupling_z[..., :1]], axis=-1)
    centre = 2.0 * coupling_x[None] + 2.0 * coupling_y[:, None] + coupling_z + upper_z
    return centre * values - coupling_z * below - upper_z * above


def operate(values, coupling_x, coupling_y, coupling_z):
    padded = jnp.pad(values, ((1, 1), (1, 1), (0, 0)))
    along_x = padded[:-2, 1:-1] + padded[2:, 1:-1]
    along_y = padded[1:-1, :-2] + padded[1:-1, 2:]
    return column_part(values, coupling_x, coupling_y, coupling_z) - coupling_x[None] * along_x - coupling_y[:, None] * along_y


def precondition(residual, inverse, coupling_x, coupling_y, coupling_z):
    def forward_step(previous, items):
        source, block = items
        fresh = relax * apply_block(block, source + coupling_x * previous)
        return fresh, fresh

    start = jnp.zeros(residual.shape[1:], jnp.float32)
    unused, half_sweep = lax.scan(forward_step, start, (residual, inverse))
    padded = jnp.pad(half_sweep, ((1, 1), (1, 1), (0, 0)))
    settled = column_part(half_sweep, coupling_x, coupling_y, coupling_z) - coupling_x[None] * padded[:-2, 1:-1]
    settled = settled - coupling_y[:, None] * (padded[1:-1, :-2] + padded[1:-1, 2:])

    def backward_step(previous, items):
        source, block, base = items
        fresh = base + relax * apply_block(block, source + coupling_x * previous)
        return fresh, fresh

    unused, result = lax.scan(backward_step, start, (residual - settled, inverse, half_sweep), reverse=True)
    return result


def reference(right_side, coupling_x, coupling_y, coupling_z, inverse):
    solution = jnp.zeros_like(right_side)
    residual = right_side
    direction = right_side
    image = right_side
    curvature = jnp.float32(1.0)
    for iteration in range(ITERS):
        precond = precondition(residual, inverse, coupling_x, coupling_y, coupling_z)
        if iteration == 0:
            direction = precond
        else:
            ratio = -jnp.sum(precond * image) / curvature
            direction = precond + ratio * direction
        image = operate(direction, coupling_x, coupling_y, coupling_z)
        projection = jnp.sum(direction * residual)
        curvature = jnp.sum(direction * image)
        step_size = projection / curvature
        solution = solution + step_size * direction
        residual = residual - step_size * image
    return solution, residual
```

```python
import jax
import jax.numpy as jnp
from jax import lax
from jax.sharding import Mesh
from jax.sharding import PartitionSpec as P

WAVE = ("wave_0", "wave_1")
PLANE = ("plane_0", "plane_1")
ALL = WAVE + PLANE
NW = 8
NP = 64

relax = 1.5


def chain_device(position):
    plane, k = divmod(position, NW)
    wave = k if plane % 2 == 0 else NW - 1 - k
    return wave * NP + plane


def swap_pairs(first):
    pairs = []
    for i in range(first, NW * NP - 1, 2):
        a, b = chain_device(i), chain_device(i + 1)
        pairs += [(a, b), (b, a)]
    return pairs


NEAR = swap_pairs(0)
FAR = swap_pairs(1)


def neighbours(values):
    near = lax.ppermute(values, ALL, NEAR)
    far = lax.ppermute(values, ALL, FAR)
    return near + far


def apply_block(block, vector):
    return jnp.einsum("ij,j->i", block, vector, precision=lax.Precision.HIGHEST)


def centre_of(cx, cy, cz):
    upper_z = jnp.concatenate([cz[:, 1:], cz[:, :1]], axis=-1)
    return 2.0 * cx + 2.0 * cy + cz + upper_z, upper_z


def column_part(values, centre, cz, upper_z):
    below = jnp.concatenate([jnp.zeros_like(values[:, :1]), values[:, :-1]], axis=-1)
    above = jnp.concatenate([values[:, 1:], jnp.zeros_like(values[:, :1])], axis=-1)
    return centre * values - cz * below - upper_z * above


def lower(values):
    return jnp.concatenate([jnp.zeros_like(values[:1]), values[:-1]], axis=0)


def upper(values):
    return jnp.concatenate([values[1:], jnp.zeros_like(values[:1])], axis=0)


def sweep(source, inverse, cx, base, reverse):
    def step(previous, items):
        s, block, b = items
        fresh = b + relax * apply_block(block, s + cx[0] * previous)
        return fresh, fresh

    _, planes = lax.scan(step, jnp.zeros_like(source[0]), (source, inverse, base), reverse=reverse)
    return planes


def on_device(right_side, coupling_x, coupling_y, coupling_z, inverse):
    odd = lax.axis_index("plane_1") % 2 == 1

    def turned(values, axis):
        return jnp.where(odd, lax.rev(values, (axis,)), values)

    extra = jnp.stack(
        [
            right_side[0],
            coupling_z[0],
            jnp.broadcast_to(coupling_y, coupling_z[0].shape),
            coupling_x,
        ],
        axis=1,
    )
    packed = turned(jnp.concatenate([inverse[0], extra], axis=1), 0)
    columns = lax.all_to_all(packed, WAVE, split_axis=0, concat_axis=0, tiled=True)
    blocks = columns[:, :128]
    r, cz, cy, cx = (columns[:, 128 + i] for i in range(4))
    centre, upper_z = centre_of(cx, cy, cz)

    def precondition(s):
        half = sweep(s, blocks, cx, jnp.zeros_like(s), False)
        near = neighbours(half)
        settled = column_part(half, centre, cz, upper_z) - cx * lower(half) - cy * near
        return sweep(s - settled, blocks, cx, half, True)

    def operate(v):
        near = neighbours(v)
        return column_part(v, centre, cz, upper_z) - cx * (lower(v) + upper(v)) - cy * near

    z = precondition(r)
    q = operate(z)
    w = precondition(q)
    p = operate(w)
    sums = jnp.stack([jnp.sum(a * b) for a, b in ((z, r), (z, q), (w, r), (w, q), (w, p))])
    sums = jnp.broadcast_to(jnp.pad(sums, (0, 123))[None], (NW, 128))
    back = lax.all_to_all(
        jnp.stack([z, q, w, p, sums], axis=1), WAVE, split_axis=0, concat_axis=0, tiled=True
    )
    part = jnp.sum(back[:, 4], axis=0)
    everyone = lax.all_to_all(
        jnp.broadcast_to(part[None, None], (NP, 1, 128)), PLANE, split_axis=0, concat_axis=0, tiled=True
    )
    total = jnp.sum(everyone[:, 0], axis=0)
    zr, zq, wr, wq, wp = (total[i] for i in range(5))
    first = zr / zq
    ratio = wq / zq
    second = (first * wq - wr) / (wp - ratio * wq)
    lead = first + second * ratio
    fields = turned(back[:, :4], 0)
    solution = lead * fields[:, 0] - second * fields[:, 2]
    residual = right_side[0] - lead * fields[:, 1] + second * fields[:, 3]
    return solution[None], residual[None]


def solution(mesh):
    torus = Mesh(mesh.devices.reshape(4, 2, 4, 16), ALL)
    return jax.shard_map(
        on_device,
        mesh=torus,
        in_specs=(
            P(WAVE, PLANE, None),
            P(PLANE, None),
            P(WAVE, None),
            P(WAVE, PLANE, None),
            P(WAVE, PLANE, None, None),
        ),
        out_specs=(P(WAVE, PLANE, None), P(WAVE, PLANE, None)),
        check_vma=False,
    )
```

```python
import jax
import jax.numpy as jnp
from jax import lax
from jax.sharding import Mesh
from jax.sharding import PartitionSpec as P

WAVE = ("wave_0", "wave_1")
PLANE = ("plane_0", "plane_1")
ALL = WAVE + PLANE
NW = 8
NP = 64

relax = 1.5


def chain_device(position):
    plane, k = divmod(position, NW)
    wave = k if plane % 2 == 0 else NW - 1 - k
    return wave * NP + plane


def swap_pairs(first):
    pairs = []
    for i in range(first, NW * NP - 1, 2):
        a, b = chain_device(i), chain_device(i + 1)
        pairs += [(a, b), (b, a)]
    return pairs


NEAR = swap_pairs(0)
FAR = swap_pairs(1)


def neighbours(values):
    far = lax.ppermute(values, ALL, FAR)
    near = lax.ppermute(values, ALL, NEAR)
    return far + near


def apply_block(block, vector):
    return jnp.einsum("ij,j->i", block, vector, precision=lax.Precision.HIGHEST)


def centre_of(cx, cy, cz):
    upper_z = jnp.concatenate([cz[:, 1:], cz[:, :1]], axis=-1)
    return 2.0 * cx + 2.0 * cy + cz + upper_z, upper_z


def column_part(values, centre, cz, upper_z):
    below = jnp.concatenate([jnp.zeros_like(values[:, :1]), values[:, :-1]], axis=-1)
    above = jnp.concatenate([values[:, 1:], jnp.zeros_like(values[:, :1])], axis=-1)
    return centre * values - cz * below - upper_z * above


def lower(values):
    return jnp.concatenate([jnp.zeros_like(values[:1]), values[:-1]], axis=0)


def upper(values):
    return jnp.concatenate([values[1:], jnp.zeros_like(values[:1])], axis=0)


def sweep(source, inverse, cx, base, reverse):
    def step(previous, items):
        s, block, b = items
        fresh = b + relax * apply_block(block, s + cx[0] * previous)
        return fresh, fresh

    _, planes = lax.scan(step, jnp.zeros_like(source[0]), (source, inverse, base), reverse=reverse)
    return planes


def on_device(right_side, coupling_x, coupling_y, coupling_z, inverse):
    odd = lax.axis_index("plane_1") % 2 == 1

    def turned(values, axis):
        return jnp.where(odd, lax.rev(values, (axis,)), values)

    extra = jnp.stack(
        [
            right_side[0],
            coupling_z[0],
            jnp.broadcast_to(coupling_y, coupling_z[0].shape),
            coupling_x,
        ],
        axis=1,
    )
    packed = turned(jnp.concatenate([inverse[0], extra], axis=1), 0)
    columns = lax.all_to_all(packed, WAVE, split_axis=0, concat_axis=0, tiled=True)
    blocks = columns[:, :128]
    r, cz, cy, cx = (columns[:, 128 + i] for i in range(4))
    centre, upper_z = centre_of(cx, cy, cz)

    def precondition(s):
        half = sweep(s, blocks, cx, jnp.zeros_like(s), False)
        near = neighbours(half)
        settled = column_part(half, centre, cz, upper_z) - cx * lower(half) - cy * near
        return sweep(s - settled, blocks, cx, half, True)

    def operate(v):
        near = neighbours(v)
        return column_part(v, centre, cz, upper_z) - cx * (lower(v) + upper(v)) - cy * near

    z = precondition(r)
    q = operate(z)
    w = precondition(q)
    p = operate(w)
    sums = jnp.stack([jnp.sum(a * b) for a, b in ((z, r), (z, q), (w, r), (w, q), (w, p))])
    sums = jnp.broadcast_to(jnp.pad(sums, (0, 123))[None], (NW, 128))
    back = lax.all_to_all(
        jnp.stack([z, q, w, p, sums], axis=1), WAVE, split_axis=0, concat_axis=0, tiled=True
    )
    part = jnp.sum(back[:, 4], axis=0)
    everyone = lax.all_to_all(
        jnp.broadcast_to(part[None, None], (NP, 1, 128)), PLANE, split_axis=0, concat_axis=0, tiled=True
    )
    total = jnp.sum(everyone[:, 0], axis=0)
    zr, zq, wr, wq, wp = (total[i] for i in range(5))
    first = zr / zq
    ratio = wq / zq
    second = (first * wq - wr) / (wp - ratio * wq)
    lead = first + second * ratio
    fields = turned(back[:, :4], 0)
    solution = lead * fields[:, 0] - second * fields[:, 2]
    residual = right_side[0] - lead * fields[:, 1] + second * fields[:, 3]
    return solution[None], residual[None]


def solution(mesh):
    torus = Mesh(mesh.devices.reshape(4, 2, 4, 16), ALL)
    return jax.shard_map(
        on_device,
        mesh=torus,
        in_specs=(
            P(WAVE, PLANE, None),
            P(PLANE, None),
            P(WAVE, None),
            P(WAVE, PLANE, None),
            P(WAVE, PLANE, None, None),
        ),
        out_specs=(P(WAVE, PLANE, None), P(WAVE, PLANE, None)),
        check_vma=False,
    )
```

```python
import jax
import jax.numpy as jnp
from jax import lax
from jax.experimental import pallas as pl
from jax.experimental.pallas import tpu as pltpu
from jax.sharding import Mesh
from jax.sharding import PartitionSpec as P

WAVE = ("wave_0", "wave_1")
PLANE = ("plane_0", "plane_1")
ALL = WAVE + PLANE
NW = 8
NP = 64
B = 128
R, CZ, CX, CY = B, B + 1, B + 2, B + 3
ROWS = B + 8

relax = 1.5

VMEM = pl.BlockSpec(memory_space=pltpu.VMEM)
HBM = pl.BlockSpec(memory_space=pl.ANY)


def chain_device(position):
    plane, k = divmod(position, NW)
    wave = k if plane % 2 == 0 else NW - 1 - k
    return wave * NP + plane


def swap_pairs(first):
    pairs = []
    for i in range(first, NW * NP - 1, 2):
        a, b = chain_device(i), chain_device(i + 1)
        pairs += [(a, b), (b, a)]
    return pairs


NEAR = swap_pairs(0)
FAR = swap_pairs(1)


def neighbours(values):
    far = lax.ppermute(values, ALL, FAR)
    near = lax.ppermute(values, ALL, NEAR)
    return far, near


def f32(*shape):
    return jax.ShapeDtypeStruct(shape, jnp.float32)


def on_chip(*shape):
    return pltpu.VMEM(shape, jnp.float32)


def turned(j):
    parity = lax.axis_index("plane_1") % 2
    return j + parity * (NW - 1 - 2 * j)


def pack_kernel(inverse, right, cz, cx, cy, packed, r_out, cz_v, cx_v, cy_v, sems, small):
    copies = [
        pltpu.make_async_copy(right.at[0], r_out, small.at[0]),
        pltpu.make_async_copy(cz.at[0], cz_v, small.at[1]),
        pltpu.make_async_copy(cx, cx_v, small.at[2]),
        pltpu.make_async_copy(cy, cy_v, small.at[3]),
    ]
    for copy in copies:
        copy.start()
    blocks = [
        pltpu.make_async_copy(inverse.at[0, j], packed.at[turned(j), 0:B, :], sems.at[j])
        for j in range(NW)
    ]
    for copy in blocks:
        copy.start()
    for copy in copies:
        copy.wait()
    r_v, cz_a, cx_a, cy_a = r_out[...], cz_v[...], cx_v[...], cy_v[...]
    for j in range(NW):
        rows = [r_v[j : j + 1], cz_a[j : j + 1], cx_a[j : j + 1], cy_a]
        rows.append(jnp.zeros((ROWS - B - 4, B), jnp.float32))
        packed[turned(j), B:ROWS, :] = jnp.concatenate(rows, axis=0)
    for copy in blocks:
        copy.wait()


def pack(inverse, right_side, coupling_z, coupling_x, coupling_y):
    return pl.pallas_call(
        pack_kernel,
        out_shape=(on_chip(NW, ROWS, B), on_chip(NW, B)),
        in_specs=[HBM] * 5,
        out_specs=(VMEM, VMEM),
        scratch_shapes=[
            pltpu.VMEM((NW, B), jnp.float32),
            pltpu.VMEM((NW, B), jnp.float32),
            pltpu.VMEM((1, B), jnp.float32),
            pltpu.SemaphoreType.DMA((NW,)),
            pltpu.SemaphoreType.DMA((4,)),
        ],
        name="pack",
    )(inverse, right_side, coupling_z, coupling_x, coupling_y)


def times_block(columns, x, vector):
    return jnp.sum(columns[x, 0:B, :] * vector, axis=1).reshape(1, B)


def forward(columns, source, out):
    cx = columns[0, CX : CX + 1, :]
    previous = None
    for x in range(NW):
        s = source(x)
        if previous is not None:
            s = s + cx * previous
        previous = relax * times_block(columns, x, s)
        out[x : x + 1, :] = previous


def first_kernel(columns, half):
    forward(columns, lambda x: columns[x, R : R + 1, :], half)


def image_kernel(columns, local, far, near, cy, image, half):
    image[...] = local[...] - cy[...] * (far[...] + near[...])
    value = image[...]
    forward(columns, lambda x: value[x : x + 1], half)


def backward_kernel(columns, base, near, far, cy, half, out):
    source = base[...] + cy[...] * (far[...] + near[...])
    cx = columns[0, CX : CX + 1, :]
    previous = None
    for x in reversed(range(NW)):
        s = source[x : x + 1]
        if previous is not None:
            s = s + cx * previous
        previous = half[x : x + 1, :] + relax * times_block(columns, x, s)
        out[x : x + 1, :] = previous


def sums_kernel(r, z, q, w, local, far, near, cy, back):
    z_a, q_a, w_a = z[...], q[...], w[...]
    p_a = local[...] - cy[...] * (far[...] + near[...])
    lane = lax.broadcasted_iota(jnp.int32, (1, B), 1)
    row = jnp.zeros((1, B), jnp.float32)
    for k, product in enumerate((z_a * r[...], z_a * q_a, w_a * r[...], w_a * q_a, w_a * p_a)):
        total = jnp.sum(jnp.sum(product, axis=0, keepdims=True), axis=1, keepdims=True)
        row = jnp.where(lane == k, total, row)
    rest = jnp.zeros((3, B), jnp.float32)
    for x in range(NW):
        at = slice(x, x + 1)
        back[x] = jnp.concatenate([z_a[at], q_a[at], w_a[at], p_a[at], row, rest], axis=0)


def share_kernel(back, out):
    part = back[0, 4:5, :]
    for x in range(1, NW):
        part = part + back[x, 4:5, :]
    out[...] = jnp.broadcast_to(part[None], (NP, 1, B))


def final_kernel(everyone, back, r, solution_out, residual_out):
    total = jnp.sum(everyone[...], axis=0)
    zr, zq, wr, wq, wp = (total[:, k : k + 1] for k in range(5))
    first = zr / zq
    ratio = wq / zq
    second = (first * wq - wr) / (wp - ratio * wq)
    lead = first + second * ratio
    for j in range(NW):
        field = back[turned(j)]
        solution_out[0, j : j + 1, :] = lead * field[0:1] - second * field[2:3]
        residual_out[0, j : j + 1, :] = r[j : j + 1] - lead * field[1:2] + second * field[3:4]


def local(kernel, out, name):
    def call(*args):
        specs = tuple(VMEM for _ in out) if isinstance(out, tuple) else VMEM
        args = [pltpu.with_memory_space_constraint(a, pltpu.VMEM) for a in args]
        return pl.pallas_call(
            kernel, out_shape=out, in_specs=[VMEM] * len(args), out_specs=specs, name=name
        )(*args)

    return call


def column_part(values, centre, cz, upper_z):
    below = jnp.concatenate([jnp.zeros_like(values[:, :1]), values[:, :-1]], axis=-1)
    above = jnp.concatenate([values[:, 1:], jnp.zeros_like(values[:, :1])], axis=-1)
    return centre * values - cz * below - upper_z * above


def lower(values):
    return jnp.concatenate([jnp.zeros_like(values[:1]), values[:-1]], axis=0)


def upper(values):
    return jnp.concatenate([values[1:], jnp.zeros_like(values[:1])], axis=0)


def on_device(right_side, coupling_x, coupling_y, coupling_z, inverse):
    packed, own = pack(inverse, right_side, coupling_z, coupling_x, coupling_y)
    columns = lax.all_to_all(packed, WAVE, split_axis=0, concat_axis=0, tiled=True)
    r, cz, cx, cy = (columns[:, i] for i in (R, CZ, CX, CY))
    upper_z = jnp.concatenate([cz[:, 1:], cz[:, :1]], axis=-1)
    centre = 2.0 * cx + 2.0 * cy + cz + upper_z

    def before(source, half):
        return source - column_part(half, centre, cz, upper_z) + cx * lower(half)

    def image_part(values):
        return column_part(values, centre, cz, upper_z) - cx * (lower(values) + upper(values))

    field = on_chip(NW, B)
    half = local(first_kernel, field, "first")(columns)
    far, near = neighbours(half)
    z = local(backward_kernel, field, "backward")(columns, before(r, half), near, far, cy, half)
    far, near = neighbours(z)
    q, half = local(image_kernel, (field, field), "image")(columns, image_part(z), far, near, cy)
    far, near = neighbours(half)
    w = local(backward_kernel, field, "backward")(columns, before(q, half), near, far, cy, half)
    far, near = neighbours(w)
    back = local(sums_kernel, on_chip(NW, 8, B), "sums")(r, z, q, w, image_part(w), far, near, cy)
    back = lax.all_to_all(back, WAVE, split_axis=0, concat_axis=0, tiled=True)
    share = local(share_kernel, on_chip(NP, 1, B), "share")(back)
    everyone = lax.all_to_all(share, PLANE, split_axis=0, concat_axis=0, tiled=True)
    out = f32(1, NW, B)
    return local(final_kernel, (out, out), "final")(everyone, back, own)


def solution(mesh):
    torus = Mesh(mesh.devices.reshape(4, 2, 4, 16), ALL)
    return jax.shard_map(
        on_device,
        mesh=torus,
        in_specs=(
            P(WAVE, PLANE, None),
            P(PLANE, None),
            P(WAVE, None),
            P(WAVE, PLANE, None),
            P(WAVE, PLANE, None, None),
        ),
        out_specs=(P(WAVE, PLANE, None), P(WAVE, PLANE, None)),
        check_vma=False,
    )
```

```python
import jax
import jax.numpy as jnp
from jax import lax
from jax.experimental import pallas as pl
from jax.experimental.pallas import tpu as pltpu
from jax.sharding import Mesh
from jax.sharding import PartitionSpec as P

WAVE = ("wave_0", "wave_1")
PLANE = ("plane_0", "plane_1")
ALL = WAVE + PLANE
NW = 8
NP = 64
B = 128
R, CZ, CX, CY = B, B + 1, B + 2, B + 3
ROWS = B + 8

relax = 1.5

VMEM = pl.BlockSpec(memory_space=pltpu.VMEM)
HBM = pl.BlockSpec(memory_space=pl.ANY)


EVEN = (7, 6, 5, 4, 3, 2, 0, 1)
ODD = EVEN[::-1]


def chain_device(position):
    plane, k = divmod(position, NW)
    return (ODD if plane % 2 else EVEN)[k] * NP + plane


def swap_pairs(first):
    pairs = []
    for i in range(first, NW * NP - 1, 2):
        a, b = chain_device(i), chain_device(i + 1)
        pairs += [(a, b), (b, a)]
    return pairs


NEAR = swap_pairs(0)
FAR = swap_pairs(1)


def neighbours(values):
    far = lax.ppermute(values, ALL, FAR)
    near = lax.ppermute(values, ALL, NEAR)
    return far, near


def f32(*shape):
    return jax.ShapeDtypeStruct(shape, jnp.float32)


def on_chip(*shape):
    return pltpu.VMEM(shape, jnp.float32)


def turned(j):
    parity = lax.axis_index("plane_1") % 2
    return EVEN[j] + parity * (ODD[j] - EVEN[j])


def pack_kernel(inverse, right, cz, cx, cy, packed, r_out, cz_v, cx_v, cy_v, sems, small):
    copies = [
        pltpu.make_async_copy(right.at[0], r_out, small.at[0]),
        pltpu.make_async_copy(cz.at[0], cz_v, small.at[1]),
        pltpu.make_async_copy(cx, cx_v, small.at[2]),
        pltpu.make_async_copy(cy, cy_v, small.at[3]),
    ]
    for copy in copies:
        copy.start()
    blocks = [
        pltpu.make_async_copy(inverse.at[0, j], packed.at[turned(j), 0:B, :], sems.at[j])
        for j in range(NW)
    ]
    for copy in blocks:
        copy.start()
    for copy in copies:
        copy.wait()
    r_v, cz_a, cx_a, cy_a = r_out[...], cz_v[...], cx_v[...], cy_v[...]
    for j in range(NW):
        rows = [r_v[j : j + 1], cz_a[j : j + 1], cx_a[j : j + 1], cy_a]
        rows.append(jnp.zeros((ROWS - B - 4, B), jnp.float32))
        packed[turned(j), B:ROWS, :] = jnp.concatenate(rows, axis=0)
    for copy in blocks:
        copy.wait()


def pack(inverse, right_side, coupling_z, coupling_x, coupling_y):
    return pl.pallas_call(
        pack_kernel,
        out_shape=(on_chip(NW, ROWS, B), on_chip(NW, B)),
        in_specs=[HBM] * 5,
        out_specs=(VMEM, VMEM),
        scratch_shapes=[
            pltpu.VMEM((NW, B), jnp.float32),
            pltpu.VMEM((NW, B), jnp.float32),
            pltpu.VMEM((1, B), jnp.float32),
            pltpu.SemaphoreType.DMA((NW,)),
            pltpu.SemaphoreType.DMA((4,)),
        ],
        name="pack",
    )(inverse, right_side, coupling_z, coupling_x, coupling_y)


def times_block(columns, x, vector):
    return jnp.sum(columns[x, 0:B, :] * vector, axis=1).reshape(1, B)


def forward(columns, source, out):
    cx = columns[0, CX : CX + 1, :]
    previous = None
    for x in range(NW):
        s = source(x)
        if previous is not None:
            s = s + cx * previous
        previous = relax * times_block(columns, x, s)
        out[x : x + 1, :] = previous


def first_kernel(columns, half):
    forward(columns, lambda x: columns[x, R : R + 1, :], half)


def image_kernel(columns, local, far, near, cy, image, half):
    image[...] = local[...] - cy[...] * (far[...] + near[...])
    value = image[...]
    forward(columns, lambda x: value[x : x + 1], half)


def backward_kernel(columns, base, near, far, cy, half, out):
    source = base[...] + cy[...] * (far[...] + near[...])
    cx = columns[0, CX : CX + 1, :]
    previous = None
    for x in reversed(range(NW)):
        s = source[x : x + 1]
        if previous is not None:
            s = s + cx * previous
        previous = half[x : x + 1, :] + relax * times_block(columns, x, s)
        out[x : x + 1, :] = previous


def sums_kernel(r, z, q, w, local, far, near, cy, back):
    z_a, q_a, w_a = z[...], q[...], w[...]
    p_a = local[...] - cy[...] * (far[...] + near[...])
    lane = lax.broadcasted_iota(jnp.int32, (1, B), 1)
    row = jnp.zeros((1, B), jnp.float32)
    for k, product in enumerate((z_a * r[...], z_a * q_a, w_a * r[...], w_a * q_a, w_a * p_a)):
        total = jnp.sum(jnp.sum(product, axis=0, keepdims=True), axis=1, keepdims=True)
        row = jnp.where(lane == k, total, row)
    rest = jnp.zeros((3, B), jnp.float32)
    for x in range(NW):
        at = slice(x, x + 1)
        back[x] = jnp.concatenate([z_a[at], q_a[at], w_a[at], p_a[at], row, rest], axis=0)


def share_kernel(back, out):
    part = back[0, 4:5, :]
    for x in range(1, NW):
        part = part + back[x, 4:5, :]
    out[...] = jnp.broadcast_to(part[None], (NP, 1, B))


def final_kernel(everyone, back, r, solution_out, residual_out):
    total = jnp.sum(everyone[...], axis=0)
    zr, zq, wr, wq, wp = (total[:, k : k + 1] for k in range(5))
    first = zr / zq
    ratio = wq / zq
    second = (first * wq - wr) / (wp - ratio * wq)
    lead = first + second * ratio
    for j in range(NW):
        field = back[turned(j)]
        solution_out[0, j : j + 1, :] = lead * field[0:1] - second * field[2:3]
        residual_out[0, j : j + 1, :] = r[j : j + 1] - lead * field[1:2] + second * field[3:4]


def local(kernel, out, name):
    def call(*args):
        specs = tuple(VMEM for _ in out) if isinstance(out, tuple) else VMEM
        args = [pltpu.with_memory_space_constraint(a, pltpu.VMEM) for a in args]
        return pl.pallas_call(
            kernel, out_shape=out, in_specs=[VMEM] * len(args), out_specs=specs, name=name
        )(*args)

    return call


def column_part(values, centre, cz, upper_z):
    below = jnp.concatenate([jnp.zeros_like(values[:, :1]), values[:, :-1]], axis=-1)
    above = jnp.concatenate([values[:, 1:], jnp.zeros_like(values[:, :1])], axis=-1)
    return centre * values - cz * below - upper_z * above


def lower(values):
    return jnp.concatenate([jnp.zeros_like(values[:1]), values[:-1]], axis=0)


def upper(values):
    return jnp.concatenate([values[1:], jnp.zeros_like(values[:1])], axis=0)


def on_device(right_side, coupling_x, coupling_y, coupling_z, inverse):
    packed, own = pack(inverse, right_side, coupling_z, coupling_x, coupling_y)
    columns = lax.all_to_all(packed, WAVE, split_axis=0, concat_axis=0, tiled=True)
    r, cz, cx, cy = (columns[:, i] for i in (R, CZ, CX, CY))
    upper_z = jnp.concatenate([cz[:, 1:], cz[:, :1]], axis=-1)
    centre = 2.0 * cx + 2.0 * cy + cz + upper_z

    def before(source, half):
        return source - column_part(half, centre, cz, upper_z) + cx * lower(half)

    def image_part(values):
        return column_part(values, centre, cz, upper_z) - cx * (lower(values) + upper(values))

    field = on_chip(NW, B)
    half = local(first_kernel, field, "first")(columns)
    far, near = neighbours(half)
    z = local(backward_kernel, field, "backward")(columns, before(r, half), near, far, cy, half)
    far, near = neighbours(z)
    q, half = local(image_kernel, (field, field), "image")(columns, image_part(z), far, near, cy)
    far, near = neighbours(half)
    w = local(backward_kernel, field, "backward")(columns, before(q, half), near, far, cy, half)
    far, near = neighbours(w)
    back = local(sums_kernel, on_chip(NW, 8, B), "sums")(r, z, q, w, image_part(w), far, near, cy)
    back = lax.all_to_all(back, WAVE, split_axis=0, concat_axis=0, tiled=True)
    share = local(share_kernel, on_chip(NP, 1, B), "share")(back)
    everyone = lax.all_to_all(share, PLANE, split_axis=0, concat_axis=0, tiled=True)
    out = f32(1, NW, B)
    return local(final_kernel, (out, out), "final")(everyone, back, own)


def solution(mesh):
    torus = Mesh(mesh.devices.reshape(4, 2, 4, 16), ALL)
    return jax.shard_map(
        on_device,
        mesh=torus,
        in_specs=(
            P(WAVE, PLANE, None),
            P(PLANE, None),
            P(WAVE, None),
            P(WAVE, PLANE, None),
            P(WAVE, PLANE, None, None),
        ),
        out_specs=(P(WAVE, PLANE, None), P(WAVE, PLANE, None)),
        check_vma=False,
    )
```

```python
import jax
import jax.numpy as jnp
from jax import lax
from jax.experimental import pallas as pl
from jax.experimental.pallas import tpu as pltpu
from jax.sharding import Mesh
from jax.sharding import PartitionSpec as P

WAVE = ("wave_0", "wave_1")
PLANE = ("plane_0", "plane_1")
ALL = WAVE + PLANE
NW = 8
NP = 64
B = 128
R, CZ, CX, CY = B, B + 1, B + 2, B + 3
ROWS = B + 8

relax = 1.5

VMEM = pl.BlockSpec(memory_space=pltpu.VMEM)
HBM = pl.BlockSpec(memory_space=pl.ANY)


EVEN = (7, 6, 5, 4, 3, 2, 0, 1)
ODD = EVEN[::-1]


def chain_device(position):
    plane, k = divmod(position, NW)
    return (ODD if plane % 2 else EVEN)[k] * NP + plane


def swap_pairs(first):
    pairs = []
    for i in range(first, NW * NP - 1, 2):
        a, b = chain_device(i), chain_device(i + 1)
        pairs += [(a, b), (b, a)]
    return pairs


NEAR = swap_pairs(0)
FAR = swap_pairs(1)


def neighbours(values):
    far = lax.ppermute(values, ALL, FAR)
    near = lax.ppermute(values, ALL, NEAR)
    return far, near


def f32(*shape):
    return jax.ShapeDtypeStruct(shape, jnp.float32)


def on_chip(*shape):
    return pltpu.VMEM(shape, jnp.float32)


def turned(j):
    parity = lax.axis_index("plane_1") % 2
    return EVEN[j] + parity * (ODD[j] - EVEN[j])


def pack_kernel(inverse, right, cz, cx, cy, packed, r_out, cz_v, cx_v, cy_v, sems, small):
    copies = [
        pltpu.make_async_copy(right.at[0], r_out, small.at[0]),
        pltpu.make_async_copy(cz.at[0], cz_v, small.at[1]),
        pltpu.make_async_copy(cx, cx_v, small.at[2]),
        pltpu.make_async_copy(cy, cy_v, small.at[3]),
    ]
    for copy in copies:
        copy.start()
    blocks = [
        pltpu.make_async_copy(inverse.at[0, j], packed.at[turned(j), 0:B, :], sems.at[j])
        for j in range(NW)
    ]
    for copy in blocks:
        copy.start()
    for copy in copies:
        copy.wait()
    r_v, cz_a, cx_a, cy_a = r_out[...], cz_v[...], cx_v[...], cy_v[...]
    for j in range(NW):
        rows = [r_v[j : j + 1], cz_a[j : j + 1], cx_a[j : j + 1], cy_a]
        rows.append(jnp.zeros((ROWS - B - 4, B), jnp.float32))
        packed[turned(j), B:ROWS, :] = jnp.concatenate(rows, axis=0)
    for copy in blocks:
        copy.wait()


def pack(inverse, right_side, coupling_z, coupling_x, coupling_y):
    return pl.pallas_call(
        pack_kernel,
        out_shape=(on_chip(NW, ROWS, B), on_chip(NW, B)),
        in_specs=[HBM] * 5,
        out_specs=(VMEM, VMEM),
        scratch_shapes=[
            pltpu.VMEM((NW, B), jnp.float32),
            pltpu.VMEM((NW, B), jnp.float32),
            pltpu.VMEM((1, B), jnp.float32),
            pltpu.SemaphoreType.DMA((NW,)),
            pltpu.SemaphoreType.DMA((4,)),
        ],
        name="pack",
    )(inverse, right_side, coupling_z, coupling_x, coupling_y)


def times_block(columns, x, vector):
    return jnp.sum(columns[x, 0:B, :] * vector, axis=1).reshape(1, B)


def forward(columns, source, out):
    cx = columns[0, CX : CX + 1, :]
    previous = None
    for x in range(NW):
        s = source(x)
        if previous is not None:
            s = s + cx * previous
        previous = relax * times_block(columns, x, s)
        out[x : x + 1, :] = previous


def first_kernel(columns, half):
    forward(columns, lambda x: columns[x, R : R + 1, :], half)


def image_kernel(columns, local, far, near, cy, image, half):
    image[...] = local[...] - cy[...] * (far[...] + near[...])
    value = image[...]
    forward(columns, lambda x: value[x : x + 1], half)


def backward_kernel(columns, base, near, far, cy, half, out):
    source = base[...] + cy[...] * (far[...] + near[...])
    cx = columns[0, CX : CX + 1, :]
    previous = None
    for x in reversed(range(NW)):
        s = source[x : x + 1]
        if previous is not None:
            s = s + cx * previous
        previous = half[x : x + 1, :] + relax * times_block(columns, x, s)
        out[x : x + 1, :] = previous


def sums_kernel(r, z, q, w, local, far, near, cy, p, share):
    z_a, q_a, w_a = z[...], q[...], w[...]
    p_a = local[...] - cy[...] * (far[...] + near[...])
    p[...] = p_a
    lane = lax.broadcasted_iota(jnp.int32, (1, B), 1)
    row = jnp.zeros((1, B), jnp.float32)
    for k, product in enumerate((z_a * r[...], z_a * q_a, w_a * r[...], w_a * q_a, w_a * p_a)):
        total = jnp.sum(jnp.sum(product, axis=0, keepdims=True), axis=1, keepdims=True)
        row = jnp.where(lane == k, total, row)
    share[...] = jnp.broadcast_to(row[None], (NP, 1, B))


def carry_kernel(everyone, z, q, w, p, back):
    row = jnp.sum(everyone[...], axis=0)
    rest = jnp.zeros((3, B), jnp.float32)
    for x in range(NW):
        at = slice(x, x + 1)
        back[x] = jnp.concatenate([z[at], q[at], w[at], p[at], row, rest], axis=0)


def final_kernel(back, r, solution_out, residual_out):
    total = back[0, 4:5, :]
    for x in range(1, NW):
        total = total + back[x, 4:5, :]
    zr, zq, wr, wq, wp = (total[:, k : k + 1] for k in range(5))
    first = zr / zq
    ratio = wq / zq
    second = (first * wq - wr) / (wp - ratio * wq)
    lead = first + second * ratio
    for j in range(NW):
        field = back[turned(j)]
        solution_out[0, j : j + 1, :] = lead * field[0:1] - second * field[2:3]
        residual_out[0, j : j + 1, :] = r[j : j + 1] - lead * field[1:2] + second * field[3:4]


def local(kernel, out, name):
    def call(*args):
        specs = tuple(VMEM for _ in out) if isinstance(out, tuple) else VMEM
        args = [pltpu.with_memory_space_constraint(a, pltpu.VMEM) for a in args]
        return pl.pallas_call(
            kernel, out_shape=out, in_specs=[VMEM] * len(args), out_specs=specs, name=name
        )(*args)

    return call


def column_part(values, centre, cz, upper_z):
    below = jnp.concatenate([jnp.zeros_like(values[:, :1]), values[:, :-1]], axis=-1)
    above = jnp.concatenate([values[:, 1:], jnp.zeros_like(values[:, :1])], axis=-1)
    return centre * values - cz * below - upper_z * above


def lower(values):
    return jnp.concatenate([jnp.zeros_like(values[:1]), values[:-1]], axis=0)


def upper(values):
    return jnp.concatenate([values[1:], jnp.zeros_like(values[:1])], axis=0)


def on_device(right_side, coupling_x, coupling_y, coupling_z, inverse):
    packed, own = pack(inverse, right_side, coupling_z, coupling_x, coupling_y)
    columns = lax.all_to_all(packed, WAVE, split_axis=0, concat_axis=0, tiled=True)
    r, cz, cx, cy = (columns[:, i] for i in (R, CZ, CX, CY))
    upper_z = jnp.concatenate([cz[:, 1:], cz[:, :1]], axis=-1)
    centre = 2.0 * cx + 2.0 * cy + cz + upper_z

    def before(source, half):
        return source - column_part(half, centre, cz, upper_z) + cx * lower(half)

    def image_part(values):
        return column_part(values, centre, cz, upper_z) - cx * (lower(values) + upper(values))

    field = on_chip(NW, B)
    half = local(first_kernel, field, "first")(columns)
    far, near = neighbours(half)
    z = local(backward_kernel, field, "backward")(columns, before(r, half), near, far, cy, half)
    far, near = neighbours(z)
    q, half = local(image_kernel, (field, field), "image")(columns, image_part(z), far, near, cy)
    far, near = neighbours(half)
    w = local(backward_kernel, field, "backward")(columns, before(q, half), near, far, cy, half)
    far, near = neighbours(w)
    sums = (field, on_chip(NP, 1, B))
    p, share = local(sums_kernel, sums, "sums")(r, z, q, w, image_part(w), far, near, cy)
    everyone = lax.all_to_all(share, PLANE, split_axis=0, concat_axis=0, tiled=True)
    back = local(carry_kernel, on_chip(NW, 8, B), "carry")(everyone, z, q, w, p)
    back = lax.all_to_all(back, WAVE, split_axis=0, concat_axis=0, tiled=True)
    out = f32(1, NW, B)
    return local(final_kernel, (out, out), "final")(back, own)


def solution(mesh):
    torus = Mesh(mesh.devices.reshape(4, 2, 4, 16), ALL)
    return jax.shard_map(
        on_device,
        mesh=torus,
        in_specs=(
            P(WAVE, PLANE, None),
            P(PLANE, None),
            P(WAVE, None),
            P(WAVE, PLANE, None),
            P(WAVE, PLANE, None, None),
        ),
        out_specs=(P(WAVE, PLANE, None), P(WAVE, PLANE, None)),
        check_vma=False,
    )
```

```python
import jax
import jax.numpy as jnp
from jax import lax
from jax.experimental import pallas as pl
from jax.experimental.pallas import tpu as pltpu
from jax.sharding import Mesh
from jax.sharding import PartitionSpec as P

WAVE = ("wave_0", "wave_1")
PLANE = ("plane_0", "plane_1")
ALL = WAVE + PLANE
NW = 8
NP = 64
B = 128
R, CZ, CX, CY = B, B + 1, B + 2, B + 3
ROWS = B + 8

relax = 1.5

VMEM = pl.BlockSpec(memory_space=pltpu.VMEM)
HBM = pl.BlockSpec(memory_space=pl.ANY)


EVEN = (7, 6, 5, 4, 3, 2, 0, 1)
ODD = EVEN[::-1]


def chain_device(position):
    plane, k = divmod(position, NW)
    return (ODD if plane % 2 else EVEN)[k] * NP + plane


def swap_pairs(first):
    pairs = []
    for i in range(first, NW * NP - 1, 2):
        a, b = chain_device(i), chain_device(i + 1)
        pairs += [(a, b), (b, a)]
    return pairs


NEAR = swap_pairs(0)
FAR = swap_pairs(1)


def neighbours(values):
    far = lax.ppermute(values, ALL, FAR)
    near = lax.ppermute(values, ALL, NEAR)
    return far, near


def f32(*shape):
    return jax.ShapeDtypeStruct(shape, jnp.float32)


def on_chip(*shape):
    return pltpu.VMEM(shape, jnp.float32)


def turned(j):
    parity = lax.axis_index("plane_1") % 2
    return EVEN[j] + parity * (ODD[j] - EVEN[j])


def pack_kernel(inverse, right, cz, cx, cy, packed, r_out, cz_v, cx_v, cy_v, sems, small):
    copies = [
        pltpu.make_async_copy(right.at[0], r_out, small.at[0]),
        pltpu.make_async_copy(cz.at[0], cz_v, small.at[1]),
        pltpu.make_async_copy(cx, cx_v, small.at[2]),
        pltpu.make_async_copy(cy, cy_v, small.at[3]),
    ]
    for copy in copies:
        copy.start()
    blocks = [
        pltpu.make_async_copy(inverse.at[0, j], packed.at[turned(j), 0:B, :], sems.at[j])
        for j in range(NW)
    ]
    for copy in blocks:
        copy.start()
    for copy in copies:
        copy.wait()
    r_v, cz_a, cx_a, cy_a = r_out[...], cz_v[...], cx_v[...], cy_v[...]
    for j in range(NW):
        rows = [r_v[j : j + 1], cz_a[j : j + 1], cx_a[j : j + 1], cy_a]
        rows.append(jnp.zeros((ROWS - B - 4, B), jnp.float32))
        packed[turned(j), B:ROWS, :] = jnp.concatenate(rows, axis=0)
    for copy in blocks:
        copy.wait()


def pack(inverse, right_side, coupling_z, coupling_x, coupling_y):
    return pl.pallas_call(
        pack_kernel,
        out_shape=(on_chip(NW, ROWS, B), on_chip(NW, B)),
        in_specs=[HBM] * 5,
        out_specs=(VMEM, VMEM),
        scratch_shapes=[
            pltpu.VMEM((NW, B), jnp.float32),
            pltpu.VMEM((NW, B), jnp.float32),
            pltpu.VMEM((1, B), jnp.float32),
            pltpu.SemaphoreType.DMA((NW,)),
            pltpu.SemaphoreType.DMA((4,)),
        ],
        name="pack",
    )(inverse, right_side, coupling_z, coupling_x, coupling_y)


def times_block(columns, x, vector):
    return jnp.sum(columns[x, 0:B, :] * vector, axis=1).reshape(1, B)


def forward(columns, source, out):
    cx = columns[0, CX : CX + 1, :]
    previous = None
    for x in range(NW):
        s = source(x)
        if previous is not None:
            s = s + cx * previous
        previous = relax * times_block(columns, x, s)
        out[x : x + 1, :] = previous


def first_kernel(columns, half):
    forward(columns, lambda x: columns[x, R : R + 1, :], half)


def image_kernel(columns, local, near, far, cy, image, half):
    image[...] = local[...] - cy[...] * (far[...] + near[...])
    value = image[...]
    forward(columns, lambda x: value[x : x + 1], half)


def backward_kernel(columns, base, near, far, cy, half, out):
    source = base[...] + cy[...] * (far[...] + near[...])
    cx = columns[0, CX : CX + 1, :]
    previous = None
    for x in reversed(range(NW)):
        s = source[x : x + 1]
        if previous is not None:
            s = s + cx * previous
        previous = half[x : x + 1, :] + relax * times_block(columns, x, s)
        out[x : x + 1, :] = previous


def sums_kernel(r, z, q, w, local, near, far, cy, p, share):
    z_a, q_a, w_a = z[...], q[...], w[...]
    p_a = local[...] - cy[...] * (far[...] + near[...])
    p[...] = p_a
    lane = lax.broadcasted_iota(jnp.int32, (1, B), 1)
    row = jnp.zeros((1, B), jnp.float32)
    for k, product in enumerate((z_a * r[...], z_a * q_a, w_a * r[...], w_a * q_a, w_a * p_a)):
        total = jnp.sum(jnp.sum(product, axis=0, keepdims=True), axis=1, keepdims=True)
        row = jnp.where(lane == k, total, row)
    share[...] = jnp.broadcast_to(row[None], (NP, 1, B))


def carry_kernel(everyone, z, q, w, p, back):
    row = jnp.sum(everyone[...], axis=0)
    rest = jnp.zeros((3, B), jnp.float32)
    for x in range(NW):
        at = slice(x, x + 1)
        back[x] = jnp.concatenate([z[at], q[at], w[at], p[at], row, rest], axis=0)


def final_kernel(back, r, solution_out, residual_out):
    total = back[0, 4:5, :]
    for x in range(1, NW):
        total = total + back[x, 4:5, :]
    zr, zq, wr, wq, wp = (total[:, k : k + 1] for k in range(5))
    first = zr / zq
    ratio = wq / zq
    second = (first * wq - wr) / (wp - ratio * wq)
    lead = first + second * ratio
    for j in range(NW):
        field = back[turned(j)]
        solution_out[0, j : j + 1, :] = lead * field[0:1] - second * field[2:3]
        residual_out[0, j : j + 1, :] = r[j : j + 1] - lead * field[1:2] + second * field[3:4]


def local(kernel, out, name):
    def call(*args):
        specs = tuple(VMEM for _ in out) if isinstance(out, tuple) else VMEM
        args = [pltpu.with_memory_space_constraint(a, pltpu.VMEM) for a in args]
        return pl.pallas_call(
            kernel, out_shape=out, in_specs=[VMEM] * len(args), out_specs=specs, name=name
        )(*args)

    return call


def column_part(values, centre, cz, upper_z):
    below = jnp.concatenate([jnp.zeros_like(values[:, :1]), values[:, :-1]], axis=-1)
    above = jnp.concatenate([values[:, 1:], jnp.zeros_like(values[:, :1])], axis=-1)
    return centre * values - cz * below - upper_z * above


def lower(values):
    return jnp.concatenate([jnp.zeros_like(values[:1]), values[:-1]], axis=0)


def upper(values):
    return jnp.concatenate([values[1:], jnp.zeros_like(values[:1])], axis=0)


def on_device(right_side, coupling_x, coupling_y, coupling_z, inverse):
    packed, own = pack(inverse, right_side, coupling_z, coupling_x, coupling_y)
    columns = lax.all_to_all(packed, WAVE, split_axis=0, concat_axis=0, tiled=True)
    r, cz, cx, cy = (columns[:, i] for i in (R, CZ, CX, CY))
    upper_z = jnp.concatenate([cz[:, 1:], cz[:, :1]], axis=-1)
    centre = 2.0 * cx + 2.0 * cy + cz + upper_z

    def before(source, half):
        return source - column_part(half, centre, cz, upper_z) + cx * lower(half)

    def image_part(values):
        return column_part(values, centre, cz, upper_z) - cx * (lower(values) + upper(values))

    field = on_chip(NW, B)
    half = local(first_kernel, field, "first")(columns)
    far, near = neighbours(half)
    z = local(backward_kernel, field, "backward")(columns, before(r, half), near, far, cy, half)
    far, near = neighbours(z)
    q, half = local(image_kernel, (field, field), "image")(columns, image_part(z), near, far, cy)
    far, near = neighbours(half)
    w = local(backward_kernel, field, "backward")(columns, before(q, half), near, far, cy, half)
    far, near = neighbours(w)
    sums = (field, on_chip(NP, 1, B))
    p, share = local(sums_kernel, sums, "sums")(r, z, q, w, image_part(w), near, far, cy)
    everyone = lax.all_to_all(share, PLANE, split_axis=0, concat_axis=0, tiled=True)
    back = local(carry_kernel, on_chip(NW, 8, B), "carry")(everyone, z, q, w, p)
    back = lax.all_to_all(back, WAVE, split_axis=0, concat_axis=0, tiled=True)
    out = f32(1, NW, B)
    return local(final_kernel, (out, out), "final")(back, own)


def solution(mesh):
    torus = Mesh(mesh.devices.reshape(4, 2, 4, 16), ALL)
    return jax.shard_map(
        on_device,
        mesh=torus,
        in_specs=(
            P(WAVE, PLANE, None),
            P(PLANE, None),
            P(WAVE, None),
            P(WAVE, PLANE, None),
            P(WAVE, PLANE, None, None),
        ),
        out_specs=(P(WAVE, PLANE, None), P(WAVE, PLANE, None)),
        check_vma=False,
    )
```

```python
import jax
import jax.numpy as jnp
from jax import lax
from jax.experimental import pallas as pl
from jax.experimental.pallas import tpu as pltpu
from jax.sharding import Mesh
from jax.sharding import PartitionSpec as P

WAVE = ("wave_0", "wave_1")
PLANE = ("plane_0", "plane_1")
ALL = WAVE + PLANE
NW = 8
NP = 64
B = 128
R, CZ, CX, CY = B, B + 1, B + 2, B + 3
ROWS = B + 8

relax = 1.5

VMEM = pl.BlockSpec(memory_space=pltpu.VMEM)
HBM = pl.BlockSpec(memory_space=pl.ANY)


EVEN = (7, 6, 5, 4, 3, 2, 0, 1)
ODD = EVEN[::-1]


def chain_device(position):
    plane, k = divmod(position, NW)
    return (ODD if plane % 2 else EVEN)[k] * NP + plane


def swap_pairs(first):
    pairs = []
    for i in range(first, NW * NP - 1, 2):
        a, b = chain_device(i), chain_device(i + 1)
        pairs += [(a, b), (b, a)]
    return pairs


NEAR = swap_pairs(0)
GROUPS = [[w * NP + (p + 40) % NP for p in range(NP)] for w in range(NW)]
FAR = swap_pairs(1)


def neighbours(values):
    far = lax.ppermute(values, ALL, FAR)
    near = lax.ppermute(values, ALL, NEAR)
    return far, near


def f32(*shape):
    return jax.ShapeDtypeStruct(shape, jnp.float32)


def on_chip(*shape):
    return pltpu.VMEM(shape, jnp.float32)


def turned(j):
    parity = lax.axis_index("plane_1") % 2
    return EVEN[j] + parity * (ODD[j] - EVEN[j])


def pack_kernel(inverse, right, cz, cx, cy, packed, r_out, cz_v, cx_v, cy_v, sems, small):
    copies = [
        pltpu.make_async_copy(right.at[0], r_out, small.at[0]),
        pltpu.make_async_copy(cz.at[0], cz_v, small.at[1]),
        pltpu.make_async_copy(cx, cx_v, small.at[2]),
        pltpu.make_async_copy(cy, cy_v, small.at[3]),
    ]
    for copy in copies:
        copy.start()
    blocks = [
        pltpu.make_async_copy(inverse.at[0, j], packed.at[turned(j), 0:B, :], sems.at[j])
        for j in range(NW)
    ]
    for copy in blocks:
        copy.start()
    for copy in copies:
        copy.wait()
    r_v, cz_a, cx_a, cy_a = r_out[...], cz_v[...], cx_v[...], cy_v[...]
    for j in range(NW):
        rows = [r_v[j : j + 1], cz_a[j : j + 1], cx_a[j : j + 1], cy_a]
        rows.append(jnp.zeros((ROWS - B - 4, B), jnp.float32))
        packed[turned(j), B:ROWS, :] = jnp.concatenate(rows, axis=0)
    for copy in blocks:
        copy.wait()


def pack(inverse, right_side, coupling_z, coupling_x, coupling_y):
    return pl.pallas_call(
        pack_kernel,
        out_shape=(on_chip(NW, ROWS, B), on_chip(NW, B)),
        in_specs=[HBM] * 5,
        out_specs=(VMEM, VMEM),
        scratch_shapes=[
            pltpu.VMEM((NW, B), jnp.float32),
            pltpu.VMEM((NW, B), jnp.float32),
            pltpu.VMEM((1, B), jnp.float32),
            pltpu.SemaphoreType.DMA((NW,)),
            pltpu.SemaphoreType.DMA((4,)),
        ],
        name="pack",
    )(inverse, right_side, coupling_z, coupling_x, coupling_y)


def times_block(columns, x, vector):
    return jnp.sum(columns[x, 0:B, :] * vector, axis=1).reshape(1, B)


def forward(columns, source, out):
    cx = columns[0, CX : CX + 1, :]
    previous = None
    for x in range(NW):
        s = source(x)
        if previous is not None:
            s = s + cx * previous
        previous = relax * times_block(columns, x, s)
        out[x : x + 1, :] = previous


def first_kernel(columns, half):
    forward(columns, lambda x: columns[x, R : R + 1, :], half)


def image_kernel(columns, local, far, near, cy, image, half):
    image[...] = local[...] - cy[...] * (far[...] + near[...])
    value = image[...]
    forward(columns, lambda x: value[x : x + 1], half)


def backward_kernel(columns, base, near, far, cy, half, out):
    source = base[...] + cy[...] * (far[...] + near[...])
    cx = columns[0, CX : CX + 1, :]
    previous = None
    for x in reversed(range(NW)):
        s = source[x : x + 1]
        if previous is not None:
            s = s + cx * previous
        previous = half[x : x + 1, :] + relax * times_block(columns, x, s)
        out[x : x + 1, :] = previous


def sums_kernel(r, z, q, w, local, far, near, cy, back):
    z_a, q_a, w_a = z[...], q[...], w[...]
    p_a = local[...] - cy[...] * (far[...] + near[...])
    lane = lax.broadcasted_iota(jnp.int32, (1, B), 1)
    row = jnp.zeros((1, B), jnp.float32)
    for k, product in enumerate((z_a * r[...], z_a * q_a, w_a * r[...], w_a * q_a, w_a * p_a)):
        total = jnp.sum(jnp.sum(product, axis=0, keepdims=True), axis=1, keepdims=True)
        row = jnp.where(lane == k, total, row)
    rest = jnp.zeros((3, B), jnp.float32)
    for x in range(NW):
        at = slice(x, x + 1)
        back[x] = jnp.concatenate([z_a[at], q_a[at], w_a[at], p_a[at], row, rest], axis=0)


def share_kernel(back, out):
    part = back[0, 4:5, :]
    for x in range(1, NW):
        part = part + back[x, 4:5, :]
    out[...] = jnp.broadcast_to(part[None], (NP, 1, B))


def final_kernel(everyone, back, r, solution_out, residual_out):
    total = jnp.sum(everyone[...], axis=0)
    zr, zq, wr, wq, wp = (total[:, k : k + 1] for k in range(5))
    first = zr / zq
    ratio = wq / zq
    second = (first * wq - wr) / (wp - ratio * wq)
    lead = first + second * ratio
    for j in range(NW):
        field = back[turned(j)]
        solution_out[0, j : j + 1, :] = lead * field[0:1] - second * field[2:3]
        residual_out[0, j : j + 1, :] = r[j : j + 1] - lead * field[1:2] + second * field[3:4]


def local(kernel, out, name):
    def call(*args):
        specs = tuple(VMEM for _ in out) if isinstance(out, tuple) else VMEM
        args = [pltpu.with_memory_space_constraint(a, pltpu.VMEM) for a in args]
        return pl.pallas_call(
            kernel, out_shape=out, in_specs=[VMEM] * len(args), out_specs=specs, name=name
        )(*args)

    return call


def column_part(values, centre, cz, upper_z):
    below = jnp.concatenate([jnp.zeros_like(values[:, :1]), values[:, :-1]], axis=-1)
    above = jnp.concatenate([values[:, 1:], jnp.zeros_like(values[:, :1])], axis=-1)
    return centre * values - cz * below - upper_z * above


def lower(values):
    return jnp.concatenate([jnp.zeros_like(values[:1]), values[:-1]], axis=0)


def upper(values):
    return jnp.concatenate([values[1:], jnp.zeros_like(values[:1])], axis=0)


def on_device(right_side, coupling_x, coupling_y, coupling_z, inverse):
    packed, own = pack(inverse, right_side, coupling_z, coupling_x, coupling_y)
    columns = lax.all_to_all(packed, WAVE, split_axis=0, concat_axis=0, tiled=True)
    r, cz, cx, cy = (columns[:, i] for i in (R, CZ, CX, CY))
    upper_z = jnp.concatenate([cz[:, 1:], cz[:, :1]], axis=-1)
    centre = 2.0 * cx + 2.0 * cy + cz + upper_z

    def before(source, half):
        return source - column_part(half, centre, cz, upper_z) + cx * lower(half)

    def image_part(values):
        return column_part(values, centre, cz, upper_z) - cx * (lower(values) + upper(values))

    field = on_chip(NW, B)
    half = local(first_kernel, field, "first")(columns)
    far, near = neighbours(half)
    z = local(backward_kernel, field, "backward")(columns, before(r, half), near, far, cy, half)
    far, near = neighbours(z)
    q, half = local(image_kernel, (field, field), "image")(columns, image_part(z), far, near, cy)
    far, near = neighbours(half)
    w = local(backward_kernel, field, "backward")(columns, before(q, half), near, far, cy, half)
    far, near = neighbours(w)
    back = local(sums_kernel, on_chip(NW, 8, B), "sums")(r, z, q, w, image_part(w), far, near, cy)
    back = lax.all_to_all(back, WAVE, split_axis=0, concat_axis=0, tiled=True)
    share = local(share_kernel, on_chip(NP, 1, B), "share")(back)
    everyone = lax.all_to_all(
        share, ALL, split_axis=0, concat_axis=0, tiled=True, axis_index_groups=GROUPS
    )
    out = f32(1, NW, B)
    return local(final_kernel, (out, out), "final")(everyone, back, own)


def solution(mesh):
    torus = Mesh(mesh.devices.reshape(4, 2, 4, 16), ALL)
    return jax.shard_map(
        on_device,
        mesh=torus,
        in_specs=(
            P(WAVE, PLANE, None),
            P(PLANE, None),
            P(WAVE, None),
            P(WAVE, PLANE, None),
            P(WAVE, PLANE, None, None),
        ),
        out_specs=(P(WAVE, PLANE, None), P(WAVE, PLANE, None)),
        check_vma=False,
    )
```

```python
import jax
import jax.numpy as jnp
from jax import lax
from jax.experimental import pallas as pl
from jax.experimental.pallas import tpu as pltpu
from jax.sharding import Mesh
from jax.sharding import PartitionSpec as P

WAVE = ("wave_0", "wave_1")
PLANE = ("plane_0", "plane_1")
ALL = WAVE + PLANE
NW = 8
NP = 64
B = 128
R, CZ, CX, CY = B, B + 1, B + 2, B + 3
ROWS = B + 8

relax = 1.5

VMEM = pl.BlockSpec(memory_space=pltpu.VMEM)
HBM = pl.BlockSpec(memory_space=pl.ANY)


EVEN = (7, 6, 5, 4, 3, 2, 0, 1)
ODD = EVEN[::-1]


def chain_device(position):
    plane, k = divmod(position, NW)
    return (ODD if plane % 2 else EVEN)[k] * NP + plane


def swap_pairs(first):
    pairs = []
    for i in range(first, NW * NP - 1, 2):
        a, b = chain_device(i), chain_device(i + 1)
        pairs += [(a, b), (b, a)]
    return pairs


NEAR = swap_pairs(0)
PLANE_GROUPS = [[w * NP + (p + 40) % NP for p in range(NP)] for w in range(NW)]
LEAD_IN = 5
LEAD_OUT = 5


def wave_groups(lead):
    return [[(w + lead) % NW * NP + p for w in range(NW)] for p in range(NP)]


def place(wave, lead):
    return (wave - lead) % NW
FAR = swap_pairs(1)


def neighbours(values):
    far = lax.ppermute(values, ALL, FAR)
    near = lax.ppermute(values, ALL, NEAR)
    return far, near


def exchanged(values, groups):
    return lax.all_to_all(
        values, ALL, split_axis=0, concat_axis=0, tiled=True, axis_index_groups=groups
    )


def f32(*shape):
    return jax.ShapeDtypeStruct(shape, jnp.float32)


def on_chip(*shape):
    return pltpu.VMEM(shape, jnp.float32)


def turned(j, lead):
    parity = lax.axis_index("plane_1") % 2
    even, odd = place(EVEN[j], lead), place(ODD[j], lead)
    return even + parity * (odd - even)


def pack_kernel(inverse, right, cz, cx, cy, packed, r_out, cz_v, cx_v, cy_v, sems, small):
    copies = [
        pltpu.make_async_copy(right.at[0], r_out, small.at[0]),
        pltpu.make_async_copy(cz.at[0], cz_v, small.at[1]),
        pltpu.make_async_copy(cx, cx_v, small.at[2]),
        pltpu.make_async_copy(cy, cy_v, small.at[3]),
    ]
    for copy in copies:
        copy.start()
    blocks = [
        pltpu.make_async_copy(inverse.at[0, j], packed.at[turned(j, LEAD_IN), 0:B, :], sems.at[j])
        for j in range(NW)
    ]
    for copy in blocks:
        copy.start()
    for copy in copies:
        copy.wait()
    r_v, cz_a, cx_a, cy_a = r_out[...], cz_v[...], cx_v[...], cy_v[...]
    for j in range(NW):
        rows = [r_v[j : j + 1], cz_a[j : j + 1], cx_a[j : j + 1], cy_a]
        rows.append(jnp.zeros((ROWS - B - 4, B), jnp.float32))
        packed[turned(j, LEAD_IN), B:ROWS, :] = jnp.concatenate(rows, axis=0)
    for copy in blocks:
        copy.wait()


def pack(inverse, right_side, coupling_z, coupling_x, coupling_y):
    return pl.pallas_call(
        pack_kernel,
        out_shape=(on_chip(NW, ROWS, B), on_chip(NW, B)),
        in_specs=[HBM] * 5,
        out_specs=(VMEM, VMEM),
        scratch_shapes=[
            pltpu.VMEM((NW, B), jnp.float32),
            pltpu.VMEM((NW, B), jnp.float32),
            pltpu.VMEM((1, B), jnp.float32),
            pltpu.SemaphoreType.DMA((NW,)),
            pltpu.SemaphoreType.DMA((4,)),
        ],
        name="pack",
    )(inverse, right_side, coupling_z, coupling_x, coupling_y)


def times_block(columns, x, vector):
    block = columns[place(x, LEAD_IN), 0:B, :]
    return jnp.sum(block * vector, axis=1).reshape(1, B)


def forward(columns, source, out):
    cx = columns[0, CX : CX + 1, :]
    previous = None
    for x in range(NW):
        s = source(x)
        if previous is not None:
            s = s + cx * previous
        previous = relax * times_block(columns, x, s)
        out[x : x + 1, :] = previous


def first_kernel(columns, half):
    forward(columns, lambda x: columns[place(x, LEAD_IN), R : R + 1, :], half)


def image_kernel(columns, local, far, near, cy, image, half):
    image[...] = local[...] - cy[...] * (far[...] + near[...])
    value = image[...]
    forward(columns, lambda x: value[x : x + 1], half)


def backward_kernel(columns, base, near, far, cy, half, out):
    source = base[...] + cy[...] * (far[...] + near[...])
    cx = columns[0, CX : CX + 1, :]
    previous = None
    for x in reversed(range(NW)):
        s = source[x : x + 1]
        if previous is not None:
            s = s + cx * previous
        previous = half[x : x + 1, :] + relax * times_block(columns, x, s)
        out[x : x + 1, :] = previous


def sums_kernel(r, z, q, w, local, far, near, cy, back):
    z_a, q_a, w_a = z[...], q[...], w[...]
    p_a = local[...] - cy[...] * (far[...] + near[...])
    lane = lax.broadcasted_iota(jnp.int32, (1, B), 1)
    row = jnp.zeros((1, B), jnp.float32)
    for k, product in enumerate((z_a * r[...], z_a * q_a, w_a * r[...], w_a * q_a, w_a * p_a)):
        total = jnp.sum(jnp.sum(product, axis=0, keepdims=True), axis=1, keepdims=True)
        row = jnp.where(lane == k, total, row)
    rest = jnp.zeros((3, B), jnp.float32)
    for x in range(NW):
        at = slice(x, x + 1)
        back[place(x, LEAD_OUT)] = jnp.concatenate([z_a[at], q_a[at], w_a[at], p_a[at], row, rest], axis=0)


def share_kernel(back, out):
    part = back[0, 4:5, :]
    for x in range(1, NW):
        part = part + back[x, 4:5, :]
    out[...] = jnp.broadcast_to(part[None], (NP, 1, B))


def final_kernel(everyone, back, r, solution_out, residual_out):
    total = jnp.sum(everyone[...], axis=0)
    zr, zq, wr, wq, wp = (total[:, k : k + 1] for k in range(5))
    first = zr / zq
    ratio = wq / zq
    second = (first * wq - wr) / (wp - ratio * wq)
    lead = first + second * ratio
    for j in range(NW):
        field = back[turned(j, LEAD_OUT)]
        solution_out[0, j : j + 1, :] = lead * field[0:1] - second * field[2:3]
        residual_out[0, j : j + 1, :] = r[j : j + 1] - lead * field[1:2] + second * field[3:4]


def local(kernel, out, name):
    def call(*args):
        specs = tuple(VMEM for _ in out) if isinstance(out, tuple) else VMEM
        args = [pltpu.with_memory_space_constraint(a, pltpu.VMEM) for a in args]
        return pl.pallas_call(
            kernel, out_shape=out, in_specs=[VMEM] * len(args), out_specs=specs, name=name
        )(*args)

    return call


def column_part(values, centre, cz, upper_z):
    below = jnp.concatenate([jnp.zeros_like(values[:, :1]), values[:, :-1]], axis=-1)
    above = jnp.concatenate([values[:, 1:], jnp.zeros_like(values[:, :1])], axis=-1)
    return centre * values - cz * below - upper_z * above


def lower(values):
    return jnp.concatenate([jnp.zeros_like(values[:1]), values[:-1]], axis=0)


def upper(values):
    return jnp.concatenate([values[1:], jnp.zeros_like(values[:1])], axis=0)


def on_device(right_side, coupling_x, coupling_y, coupling_z, inverse):
    packed, own = pack(inverse, right_side, coupling_z, coupling_x, coupling_y)
    columns = exchanged(packed, wave_groups(LEAD_IN))
    r, cz, cx, cy = (jnp.roll(columns[:, i], LEAD_IN, axis=0) for i in (R, CZ, CX, CY))
    upper_z = jnp.concatenate([cz[:, 1:], cz[:, :1]], axis=-1)
    centre = 2.0 * cx + 2.0 * cy + cz + upper_z

    def before(source, half):
        return source - column_part(half, centre, cz, upper_z) + cx * lower(half)

    def image_part(values):
        return column_part(values, centre, cz, upper_z) - cx * (lower(values) + upper(values))

    field = on_chip(NW, B)
    half = local(first_kernel, field, "first")(columns)
    far, near = neighbours(half)
    z = local(backward_kernel, field, "backward")(columns, before(r, half), near, far, cy, half)
    far, near = neighbours(z)
    q, half = local(image_kernel, (field, field), "image")(columns, image_part(z), far, near, cy)
    far, near = neighbours(half)
    w = local(backward_kernel, field, "backward")(columns, before(q, half), near, far, cy, half)
    far, near = neighbours(w)
    back = local(sums_kernel, on_chip(NW, 8, B), "sums")(r, z, q, w, image_part(w), far, near, cy)
    back = exchanged(back, wave_groups(LEAD_OUT))
    share = local(share_kernel, on_chip(NP, 1, B), "share")(back)
    everyone = exchanged(share, PLANE_GROUPS)
    out = f32(1, NW, B)
    return local(final_kernel, (out, out), "final")(everyone, back, own)


def solution(mesh):
    torus = Mesh(mesh.devices.reshape(4, 2, 4, 16), ALL)
    return jax.shard_map(
        on_device,
        mesh=torus,
        in_specs=(
            P(WAVE, PLANE, None),
            P(PLANE, None),
            P(WAVE, None),
            P(WAVE, PLANE, None),
            P(WAVE, PLANE, None, None),
        ),
        out_specs=(P(WAVE, PLANE, None), P(WAVE, PLANE, None)),
        check_vma=False,
    )
```

```python
import jax
import jax.numpy as jnp
from jax import lax
from jax.experimental import pallas as pl
from jax.experimental.pallas import tpu as pltpu
from jax.sharding import Mesh
from jax.sharding import PartitionSpec as P

WAVE = ("wave_0", "wave_1")
PLANE = ("plane_0", "plane_1")
ALL = WAVE + PLANE
NW = 8
NP = 64
B = 128
R, CZ, CX, CY = B, B + 1, B + 2, B + 3
ROWS = B + 8

relax = 1.5

VMEM = pl.BlockSpec(memory_space=pltpu.VMEM)
HBM = pl.BlockSpec(memory_space=pl.ANY)


EVEN = (7, 6, 5, 4, 3, 2, 0, 1)
ODD = EVEN[::-1]


def chain_device(position):
    plane, k = divmod(position, NW)
    return (ODD if plane % 2 else EVEN)[k] * NP + plane


def swap_pairs(first):
    pairs = []
    for i in range(first, NW * NP - 1, 2):
        a, b = chain_device(i), chain_device(i + 1)
        pairs += [(a, b), (b, a)]
    return pairs


NEAR = swap_pairs(0)
PLANE_GROUPS = [[w * NP + (p + 40) % NP for p in range(NP)] for w in range(NW)]
ORDER = (5, 6, 7, 0, 1, 2, 3, 4)
WAVE_GROUPS = [[w * NP + p for w in ORDER] for p in range(NP)]
PLACE = tuple(ORDER.index(w) for w in range(NW))
FAR = swap_pairs(1)


def neighbours(values):
    far = lax.ppermute(values, ALL, FAR)
    near = lax.ppermute(values, ALL, NEAR)
    return far, near


def exchanged(values, groups):
    return lax.all_to_all(
        values, ALL, split_axis=0, concat_axis=0, tiled=True, axis_index_groups=groups
    )


def f32(*shape):
    return jax.ShapeDtypeStruct(shape, jnp.float32)


def on_chip(*shape):
    return pltpu.VMEM(shape, jnp.float32)


def turned(j):
    parity = lax.axis_index("plane_1") % 2
    even, odd = PLACE[EVEN[j]], PLACE[ODD[j]]
    return even + parity * (odd - even)


def pack_kernel(inverse, right, cz, cx, cy, packed, r_out, cz_v, cx_v, cy_v, sems, small):
    copies = [
        pltpu.make_async_copy(right.at[0], r_out, small.at[0]),
        pltpu.make_async_copy(cz.at[0], cz_v, small.at[1]),
        pltpu.make_async_copy(cx, cx_v, small.at[2]),
        pltpu.make_async_copy(cy, cy_v, small.at[3]),
    ]
    for copy in copies:
        copy.start()
    blocks = [
        pltpu.make_async_copy(inverse.at[0, j], packed.at[turned(j), 0:B, :], sems.at[j])
        for j in range(NW)
    ]
    for copy in blocks:
        copy.start()
    for copy in copies:
        copy.wait()
    r_v, cz_a, cx_a, cy_a = r_out[...], cz_v[...], cx_v[...], cy_v[...]
    for j in range(NW):
        rows = [r_v[j : j + 1], cz_a[j : j + 1], cx_a[j : j + 1], cy_a]
        rows.append(jnp.zeros((ROWS - B - 4, B), jnp.float32))
        packed[turned(j), B:ROWS, :] = jnp.concatenate(rows, axis=0)
    for copy in blocks:
        copy.wait()


def pack(inverse, right_side, coupling_z, coupling_x, coupling_y):
    return pl.pallas_call(
        pack_kernel,
        out_shape=(on_chip(NW, ROWS, B), on_chip(NW, B)),
        in_specs=[HBM] * 5,
        out_specs=(VMEM, VMEM),
        scratch_shapes=[
            pltpu.VMEM((NW, B), jnp.float32),
            pltpu.VMEM((NW, B), jnp.float32),
            pltpu.VMEM((1, B), jnp.float32),
            pltpu.SemaphoreType.DMA((NW,)),
            pltpu.SemaphoreType.DMA((4,)),
        ],
        name="pack",
    )(inverse, right_side, coupling_z, coupling_x, coupling_y)


def times_block(columns, x, vector):
    block = columns[PLACE[x], 0:B, :]
    return jnp.sum(block * vector, axis=1).reshape(1, B)


def forward(columns, source, out):
    cx = columns[0, CX : CX + 1, :]
    previous = None
    for x in range(NW):
        s = source(x)
        if previous is not None:
            s = s + cx * previous
        previous = relax * times_block(columns, x, s)
        out[x : x + 1, :] = previous


def first_kernel(columns, half):
    forward(columns, lambda x: columns[PLACE[x], R : R + 1, :], half)


def image_kernel(columns, local, near, far, cy, image, half):
    image[...] = local[...] - cy[...] * (far[...] + near[...])
    value = image[...]
    forward(columns, lambda x: value[x : x + 1], half)


def column_part(values, centre, cz, upper_z):
    lane = lax.broadcasted_iota(jnp.int32, values.shape, 1)
    below = jnp.where(lane == 0, 0.0, pltpu.roll(values, 1, 1))
    above = jnp.where(lane == B - 1, 0.0, pltpu.roll(values, B - 1, 1))
    return centre * values - cz * below - upper_z * above


def lower(values):
    return jnp.concatenate([jnp.zeros((1, B), jnp.float32), values[:-1]], axis=0)


def upper(values):
    return jnp.concatenate([values[1:], jnp.zeros((1, B), jnp.float32)], axis=0)


def source_part(source, half, cx, cz, upper_z, centre):
    return source - column_part(half, centre, cz, upper_z) + cx * lower(half)


def settle_first_kernel(columns, half, base, r, faces, cy):
    rows = [
        jnp.concatenate([columns[PLACE[x], i : i + 1, :] for x in range(NW)], axis=0)
        for i in (R, CX, CZ, CY)
    ]
    upper_z = pltpu.roll(rows[2], B - 1, 1)
    centre = 2.0 * rows[1] + 2.0 * rows[3] + rows[2] + upper_z
    r[...] = rows[0]
    cy[...] = rows[3]
    for k, face in enumerate((rows[1], rows[2], upper_z, centre)):
        faces[k] = face
    base[...] = source_part(rows[0], half[...], rows[1], rows[2], upper_z, centre)


def settle_kernel(source, half, faces, base):
    base[...] = source_part(source[...], half[...], *(faces[k] for k in range(4)))


def image_part_kernel(values, faces, out):
    v = values[...]
    out[...] = column_part(v, faces[3], faces[1], faces[2]) - faces[0] * (lower(v) + upper(v))


def backward_kernel(columns, base, near, far, cy, half, out):
    source = base[...] + cy[...] * (far[...] + near[...])
    cx = columns[0, CX : CX + 1, :]
    previous = None
    for x in reversed(range(NW)):
        s = source[x : x + 1]
        if previous is not None:
            s = s + cx * previous
        previous = half[x : x + 1, :] + relax * times_block(columns, x, s)
        out[x : x + 1, :] = previous


def sums_kernel(r, z, q, w, local, near, far, cy, back):
    z_a, q_a, w_a = z[...], q[...], w[...]
    p_a = local[...] - cy[...] * (far[...] + near[...])
    lane = lax.broadcasted_iota(jnp.int32, (1, B), 1)
    row = jnp.zeros((1, B), jnp.float32)
    for k, product in enumerate((z_a * r[...], z_a * q_a, w_a * r[...], w_a * q_a, w_a * p_a)):
        total = jnp.sum(jnp.sum(product, axis=0, keepdims=True), axis=1, keepdims=True)
        row = jnp.where(lane == k, total, row)
    rest = jnp.zeros((3, B), jnp.float32)
    for x in range(NW):
        at = slice(x, x + 1)
        back[PLACE[x]] = jnp.concatenate([z_a[at], q_a[at], w_a[at], p_a[at], row, rest], axis=0)


def share_kernel(back, out):
    part = back[0, 4:5, :]
    for x in range(1, NW):
        part = part + back[x, 4:5, :]
    out[...] = jnp.broadcast_to(part[None], (NP, 1, B))


def final_kernel(everyone, back, r, solution_out, residual_out):
    total = jnp.sum(everyone[...], axis=0)
    zr, zq, wr, wq, wp = (total[:, k : k + 1] for k in range(5))
    first = zr / zq
    ratio = wq / zq
    second = (first * wq - wr) / (wp - ratio * wq)
    lead = first + second * ratio
    for j in range(NW):
        field = back[turned(j)]
        solution_out[0, j : j + 1, :] = lead * field[0:1] - second * field[2:3]
        residual_out[0, j : j + 1, :] = r[j : j + 1] - lead * field[1:2] + second * field[3:4]


def local(kernel, out, name):
    def call(*args):
        specs = tuple(VMEM for _ in out) if isinstance(out, tuple) else VMEM
        args = [pltpu.with_memory_space_constraint(a, pltpu.VMEM) for a in args]
        return pl.pallas_call(
            kernel, out_shape=out, in_specs=[VMEM] * len(args), out_specs=specs, name=name
        )(*args)

    return call


def on_device(right_side, coupling_x, coupling_y, coupling_z, inverse):
    packed, own = pack(inverse, right_side, coupling_z, coupling_x, coupling_y)
    columns = exchanged(packed, WAVE_GROUPS)
    field = on_chip(NW, B)

    def image_part(values):
        return local(image_part_kernel, field, "image_part")(values, faces)

    half = local(first_kernel, field, "first")(columns)
    far, near = neighbours(half)
    parts = (field, field, on_chip(4, NW, B), field)
    base, r, faces, cy = local(settle_first_kernel, parts, "settle_first")(columns, half)
    z = local(backward_kernel, field, "backward")(columns, base, near, far, cy, half)
    far, near = neighbours(z)
    q, half = local(image_kernel, (field, field), "image")(columns, image_part(z), near, far, cy)
    far, near = neighbours(half)
    base = local(settle_kernel, field, "settle")(q, half, faces)
    w = local(backward_kernel, field, "backward")(columns, base, near, far, cy, half)
    far, near = neighbours(w)
    back = local(sums_kernel, on_chip(NW, 8, B), "sums")(r, z, q, w, image_part(w), near, far, cy)
    back = exchanged(back, WAVE_GROUPS)
    share = local(share_kernel, on_chip(NP, 1, B), "share")(back)
    everyone = exchanged(share, PLANE_GROUPS)
    out = f32(1, NW, B)
    return local(final_kernel, (out, out), "final")(everyone, back, own)


def solution(mesh):
    torus = Mesh(mesh.devices.reshape(4, 2, 4, 16), ALL)
    return jax.shard_map(
        on_device,
        mesh=torus,
        in_specs=(
            P(WAVE, PLANE, None),
            P(PLANE, None),
            P(WAVE, None),
            P(WAVE, PLANE, None),
            P(WAVE, PLANE, None, None),
        ),
        out_specs=(P(WAVE, PLANE, None), P(WAVE, PLANE, None)),
        check_vma=False,
    )
```

```python
import jax
import jax.numpy as jnp
from jax import lax
from jax.experimental import pallas as pl
from jax.experimental.pallas import tpu as pltpu
from jax.sharding import Mesh
from jax.sharding import PartitionSpec as P

WAVE = ("wave_0", "wave_1")
PLANE = ("plane_0", "plane_1")
ALL = WAVE + PLANE
NW = 8
NP = 64
B = 128
R, CZ, CX, CY = B, B + 1, B + 2, B + 3
ROWS = B + 8

relax = 1.5

VMEM = pl.BlockSpec(memory_space=pltpu.VMEM)
HBM = pl.BlockSpec(memory_space=pl.ANY)


EVEN = (7, 6, 5, 4, 3, 2, 0, 1)
ODD = EVEN[::-1]


def chain_device(position):
    plane, k = divmod(position, NW)
    return (ODD if plane % 2 else EVEN)[k] * NP + plane


def swap_pairs(first):
    pairs = []
    for i in range(first, NW * NP - 1, 2):
        a, b = chain_device(i), chain_device(i + 1)
        pairs += [(a, b), (b, a)]
    return pairs


NEAR = swap_pairs(0)
ORDER = (5, 6, 7, 0, 1, 2, 3, 4)
WAVE_GROUPS = [[w * NP + p for w in ORDER] for p in range(NP)]
PLACE = tuple(ORDER.index(w) for w in range(NW))
NY = 4
NZ = NP // NY
SLAB_GROUPS = [
    [w * NP + (y + 2) % NY * NZ + z for y in range(NY) for w in ORDER] for z in range(NZ)
]
RING_GROUPS = [
    [w * NP + y * NZ + (z + 8) % NZ for z in range(NZ)] for w in range(NW) for y in range(NY)
]
FAR = swap_pairs(1)


def neighbours(values):
    far = lax.ppermute(values, ALL, FAR)
    near = lax.ppermute(values, ALL, NEAR)
    return far, near


def exchanged(values, groups):
    return lax.all_to_all(
        values, ALL, split_axis=0, concat_axis=0, tiled=True, axis_index_groups=groups
    )


def f32(*shape):
    return jax.ShapeDtypeStruct(shape, jnp.float32)


def on_chip(*shape):
    return pltpu.VMEM(shape, jnp.float32)


def turned(j):
    parity = lax.axis_index("plane_1") % 2
    even, odd = PLACE[EVEN[j]], PLACE[ODD[j]]
    return even + parity * (odd - even)


def pack_kernel(inverse, right, cz, cx, cy, packed, r_out, cz_v, cx_v, cy_v, sems, small):
    copies = [
        pltpu.make_async_copy(right.at[0], r_out, small.at[0]),
        pltpu.make_async_copy(cz.at[0], cz_v, small.at[1]),
        pltpu.make_async_copy(cx, cx_v, small.at[2]),
        pltpu.make_async_copy(cy, cy_v, small.at[3]),
    ]
    for copy in copies:
        copy.start()
    blocks = [
        pltpu.make_async_copy(inverse.at[0, j], packed.at[turned(j), 0:B, :], sems.at[j])
        for j in range(NW)
    ]
    for copy in blocks:
        copy.start()
    for copy in copies:
        copy.wait()
    r_v, cz_a, cx_a, cy_a = r_out[...], cz_v[...], cx_v[...], cy_v[...]
    for j in range(NW):
        rows = [r_v[j : j + 1], cz_a[j : j + 1], cx_a[j : j + 1], cy_a]
        rows.append(jnp.zeros((ROWS - B - 4, B), jnp.float32))
        packed[turned(j), B:ROWS, :] = jnp.concatenate(rows, axis=0)
    for copy in blocks:
        copy.wait()


def pack(inverse, right_side, coupling_z, coupling_x, coupling_y):
    return pl.pallas_call(
        pack_kernel,
        out_shape=(on_chip(NW, ROWS, B), on_chip(NW, B)),
        in_specs=[HBM] * 5,
        out_specs=(VMEM, VMEM),
        scratch_shapes=[
            pltpu.VMEM((NW, B), jnp.float32),
            pltpu.VMEM((NW, B), jnp.float32),
            pltpu.VMEM((1, B), jnp.float32),
            pltpu.SemaphoreType.DMA((NW,)),
            pltpu.SemaphoreType.DMA((4,)),
        ],
        name="pack",
    )(inverse, right_side, coupling_z, coupling_x, coupling_y)


def times_block(columns, x, vector):
    block = columns[PLACE[x], 0:B, :]
    return jnp.sum(block * vector, axis=1).reshape(1, B)


def forward(columns, source, out):
    cx = columns[0, CX : CX + 1, :]
    previous = None
    for x in range(NW):
        s = source(x)
        if previous is not None:
            s = s + cx * previous
        previous = relax * times_block(columns, x, s)
        out[x : x + 1, :] = previous


def first_kernel(columns, half):
    forward(columns, lambda x: columns[PLACE[x], R : R + 1, :], half)


def image_kernel(columns, local, near, far, cy, image, half):
    image[...] = local[...] - cy[...] * (far[...] + near[...])
    value = image[...]
    forward(columns, lambda x: value[x : x + 1], half)


def column_part(values, centre, cz, upper_z):
    lane = lax.broadcasted_iota(jnp.int32, values.shape, 1)
    below = jnp.where(lane == 0, 0.0, pltpu.roll(values, 1, 1))
    above = jnp.where(lane == B - 1, 0.0, pltpu.roll(values, B - 1, 1))
    return centre * values - cz * below - upper_z * above


def lower(values):
    return jnp.concatenate([jnp.zeros((1, B), jnp.float32), values[:-1]], axis=0)


def upper(values):
    return jnp.concatenate([values[1:], jnp.zeros((1, B), jnp.float32)], axis=0)


def source_part(source, half, cx, cz, upper_z, centre):
    return source - column_part(half, centre, cz, upper_z) + cx * lower(half)


def settle_first_kernel(columns, half, base, r, faces, cy):
    rows = [
        jnp.concatenate([columns[PLACE[x], i : i + 1, :] for x in range(NW)], axis=0)
        for i in (R, CX, CZ, CY)
    ]
    upper_z = pltpu.roll(rows[2], B - 1, 1)
    centre = 2.0 * rows[1] + 2.0 * rows[3] + rows[2] + upper_z
    r[...] = rows[0]
    cy[...] = rows[3]
    for k, face in enumerate((rows[1], rows[2], upper_z, centre)):
        faces[k] = face
    base[...] = source_part(rows[0], half[...], rows[1], rows[2], upper_z, centre)


def settle_kernel(source, half, faces, base):
    base[...] = source_part(source[...], half[...], *(faces[k] for k in range(4)))


def image_part_kernel(values, faces, out):
    v = values[...]
    out[...] = column_part(v, faces[3], faces[1], faces[2]) - faces[0] * (lower(v) + upper(v))


def backward_kernel(columns, base, near, far, cy, half, out):
    source = base[...] + cy[...] * (far[...] + near[...])
    cx = columns[0, CX : CX + 1, :]
    previous = None
    for x in reversed(range(NW)):
        s = source[x : x + 1]
        if previous is not None:
            s = s + cx * previous
        previous = half[x : x + 1, :] + relax * times_block(columns, x, s)
        out[x : x + 1, :] = previous


def sums_kernel(r, z, q, w, local, near, far, cy, back):
    z_a, q_a, w_a = z[...], q[...], w[...]
    p_a = local[...] - cy[...] * (far[...] + near[...])
    lane = lax.broadcasted_iota(jnp.int32, (1, B), 1)
    row = jnp.zeros((1, B), jnp.float32)
    for k, product in enumerate((z_a * r[...], z_a * q_a, w_a * r[...], w_a * q_a, w_a * p_a)):
        total = jnp.sum(jnp.sum(product, axis=0, keepdims=True), axis=1, keepdims=True)
        row = jnp.where(lane == k, total, row)
    rest = jnp.zeros((3, B), jnp.float32)
    for x in range(NW):
        at = slice(x, x + 1)
        tile = jnp.concatenate([z_a[at], q_a[at], w_a[at], p_a[at], row, rest], axis=0)
        for y in range(NY):
            back[y * NW + PLACE[x]] = tile


def share_kernel(back, out):
    part = back[0, 4:5, :]
    for x in range(1, NY * NW):
        part = part + back[x, 4:5, :]
    out[...] = jnp.broadcast_to(part[None], (NZ, 1, B))


def final_kernel(everyone, back, r, solution_out, residual_out):
    total = jnp.sum(everyone[...], axis=0)
    zr, zq, wr, wq, wp = (total[:, k : k + 1] for k in range(5))
    first = zr / zq
    ratio = wq / zq
    second = (first * wq - wr) / (wp - ratio * wq)
    lead = first + second * ratio
    slab = (lax.axis_index("plane_0") + NY - 2) % NY * NW
    for j in range(NW):
        field = back[slab + turned(j)]
        solution_out[0, j : j + 1, :] = lead * field[0:1] - second * field[2:3]
        residual_out[0, j : j + 1, :] = r[j : j + 1] - lead * field[1:2] + second * field[3:4]


def local(kernel, out, name):
    def call(*args):
        specs = tuple(VMEM for _ in out) if isinstance(out, tuple) else VMEM
        args = [pltpu.with_memory_space_constraint(a, pltpu.VMEM) for a in args]
        return pl.pallas_call(
            kernel, out_shape=out, in_specs=[VMEM] * len(args), out_specs=specs, name=name
        )(*args)

    return call


def on_device(right_side, coupling_x, coupling_y, coupling_z, inverse):
    packed, own = pack(inverse, right_side, coupling_z, coupling_x, coupling_y)
    columns = exchanged(packed, WAVE_GROUPS)
    field = on_chip(NW, B)

    def image_part(values):
        return local(image_part_kernel, field, "image_part")(values, faces)

    half = local(first_kernel, field, "first")(columns)
    far, near = neighbours(half)
    parts = (field, field, on_chip(4, NW, B), field)
    base, r, faces, cy = local(settle_first_kernel, parts, "settle_first")(columns, half)
    z = local(backward_kernel, field, "backward")(columns, base, near, far, cy, half)
    far, near = neighbours(z)
    q, half = local(image_kernel, (field, field), "image")(columns, image_part(z), near, far, cy)
    far, near = neighbours(half)
    base = local(settle_kernel, field, "settle")(q, half, faces)
    w = local(backward_kernel, field, "backward")(columns, base, near, far, cy, half)
    far, near = neighbours(w)
    back = local(sums_kernel, on_chip(NY * NW, 8, B), "sums")(r, z, q, w, image_part(w), near, far, cy)
    back = exchanged(back, SLAB_GROUPS)
    share = local(share_kernel, on_chip(NZ, 1, B), "share")(back)
    everyone = exchanged(share, RING_GROUPS)
    out = f32(1, NW, B)
    return local(final_kernel, (out, out), "final")(everyone, back, own)


def solution(mesh):
    torus = Mesh(mesh.devices.reshape(4, 2, 4, 16), ALL)
    return jax.shard_map(
        on_device,
        mesh=torus,
        in_specs=(
            P(WAVE, PLANE, None),
            P(PLANE, None),
            P(WAVE, None),
            P(WAVE, PLANE, None),
            P(WAVE, PLANE, None, None),
        ),
        out_specs=(P(WAVE, PLANE, None), P(WAVE, PLANE, None)),
        check_vma=False,
    )
```

```python
import jax
import jax.numpy as jnp
from jax import lax
from jax.experimental import pallas as pl
from jax.experimental.pallas import tpu as pltpu
from jax.sharding import Mesh
from jax.sharding import PartitionSpec as P

WAVE = ("wave_0", "wave_1")
PLANE = ("plane_0", "plane_1")
ALL = WAVE + PLANE
NW = 8
NP = 64
B = 128
R, CZ, CX, CY = B, B + 1, B + 2, B + 3
ROWS = B + 8

relax = 1.5

VMEM = pl.BlockSpec(memory_space=pltpu.VMEM)
HBM = pl.BlockSpec(memory_space=pl.ANY)


EVEN = (7, 6, 5, 4, 3, 2, 0, 1)
ODD = EVEN[::-1]


def chain_device(position):
    plane, k = divmod(position, NW)
    return (ODD if plane % 2 else EVEN)[k] * NP + plane


def swap_pairs(first):
    pairs = []
    for i in range(first, NW * NP - 1, 2):
        a, b = chain_device(i), chain_device(i + 1)
        pairs += [(a, b), (b, a)]
    return pairs


ORDER = (5, 6, 7, 0, 1, 2, 3, 4)
WAVE_GROUPS = [[w * NP + p for w in ORDER] for p in range(NP)]
PLACE = tuple(ORDER.index(w) for w in range(NW))
NY = 4
NZ = NP // NY
SLAB_GROUPS = [
    [w * NP + (y + 2) % NY * NZ + z for y in range(NY) for w in ORDER] for z in range(NZ)
]
RING_GROUPS = [
    [w * NP + y * NZ + (z + 8) % NZ for z in range(NZ)] for w in range(NW) for y in range(NY)
]
FAR = swap_pairs(1)


def neighbours(values):
    far = lax.ppermute(values, ALL, FAR)
    near = lax.psum(values, "wave_1") - values
    return far, near


def exchanged(values, groups):
    return lax.all_to_all(
        values, ALL, split_axis=0, concat_axis=0, tiled=True, axis_index_groups=groups
    )


def f32(*shape):
    return jax.ShapeDtypeStruct(shape, jnp.float32)


def on_chip(*shape):
    return pltpu.VMEM(shape, jnp.float32)


def turned(j):
    parity = lax.axis_index("plane_1") % 2
    even, odd = PLACE[EVEN[j]], PLACE[ODD[j]]
    return even + parity * (odd - even)


def pack_kernel(inverse, right, cz, cx, cy, packed, r_out, cz_v, cx_v, cy_v, sems, small):
    copies = [
        pltpu.make_async_copy(right.at[0], r_out, small.at[0]),
        pltpu.make_async_copy(cz.at[0], cz_v, small.at[1]),
        pltpu.make_async_copy(cx, cx_v, small.at[2]),
        pltpu.make_async_copy(cy, cy_v, small.at[3]),
    ]
    for copy in copies:
        copy.start()
    blocks = [
        pltpu.make_async_copy(inverse.at[0, j], packed.at[turned(j), 0:B, :], sems.at[j])
        for j in range(NW)
    ]
    for copy in blocks:
        copy.start()
    for copy in copies:
        copy.wait()
    r_v, cz_a, cx_a, cy_a = r_out[...], cz_v[...], cx_v[...], cy_v[...]
    for j in range(NW):
        rows = [r_v[j : j + 1], cz_a[j : j + 1], cx_a[j : j + 1], cy_a]
        rows.append(jnp.zeros((ROWS - B - 4, B), jnp.float32))
        packed[turned(j), B:ROWS, :] = jnp.concatenate(rows, axis=0)
    for copy in blocks:
        copy.wait()


def pack(inverse, right_side, coupling_z, coupling_x, coupling_y):
    return pl.pallas_call(
        pack_kernel,
        out_shape=(on_chip(NW, ROWS, B), on_chip(NW, B)),
        in_specs=[HBM] * 5,
        out_specs=(VMEM, VMEM),
        scratch_shapes=[
            pltpu.VMEM((NW, B), jnp.float32),
            pltpu.VMEM((NW, B), jnp.float32),
            pltpu.VMEM((1, B), jnp.float32),
            pltpu.SemaphoreType.DMA((NW,)),
            pltpu.SemaphoreType.DMA((4,)),
        ],
        name="pack",
    )(inverse, right_side, coupling_z, coupling_x, coupling_y)


def times_block(columns, x, vector):
    block = columns[PLACE[x], 0:B, :]
    return jnp.sum(block * vector, axis=1).reshape(1, B)


def forward(columns, source, out):
    cx = columns[0, CX : CX + 1, :]
    previous = None
    for x in range(NW):
        s = source(x)
        if previous is not None:
            s = s + cx * previous
        previous = relax * times_block(columns, x, s)
        out[x : x + 1, :] = previous


def first_kernel(columns, half):
    forward(columns, lambda x: columns[PLACE[x], R : R + 1, :], half)


def image_kernel(columns, local, near, far, cy, image, half):
    image[...] = local[...] - cy[...] * (far[...] + near[...])
    value = image[...]
    forward(columns, lambda x: value[x : x + 1], half)


def column_part(values, centre, cz, upper_z):
    lane = lax.broadcasted_iota(jnp.int32, values.shape, 1)
    below = jnp.where(lane == 0, 0.0, pltpu.roll(values, 1, 1))
    above = jnp.where(lane == B - 1, 0.0, pltpu.roll(values, B - 1, 1))
    return centre * values - cz * below - upper_z * above


def lower(values):
    return jnp.concatenate([jnp.zeros((1, B), jnp.float32), values[:-1]], axis=0)


def upper(values):
    return jnp.concatenate([values[1:], jnp.zeros((1, B), jnp.float32)], axis=0)


def source_part(source, half, cx, cz, upper_z, centre):
    return source - column_part(half, centre, cz, upper_z) + cx * lower(half)


def settle_first_kernel(columns, half, base, r, faces, cy):
    rows = [
        jnp.concatenate([columns[PLACE[x], i : i + 1, :] for x in range(NW)], axis=0)
        for i in (R, CX, CZ, CY)
    ]
    upper_z = pltpu.roll(rows[2], B - 1, 1)
    centre = 2.0 * rows[1] + 2.0 * rows[3] + rows[2] + upper_z
    r[...] = rows[0]
    cy[...] = rows[3]
    for k, face in enumerate((rows[1], rows[2], upper_z, centre)):
        faces[k] = face
    base[...] = source_part(rows[0], half[...], rows[1], rows[2], upper_z, centre)


def settle_kernel(source, half, faces, base):
    base[...] = source_part(source[...], half[...], *(faces[k] for k in range(4)))


def image_part_kernel(values, faces, out):
    v = values[...]
    out[...] = column_part(v, faces[3], faces[1], faces[2]) - faces[0] * (lower(v) + upper(v))


def backward_kernel(columns, base, near, far, cy, half, out):
    source = base[...] + cy[...] * (far[...] + near[...])
    cx = columns[0, CX : CX + 1, :]
    previous = None
    for x in reversed(range(NW)):
        s = source[x : x + 1]
        if previous is not None:
            s = s + cx * previous
        previous = half[x : x + 1, :] + relax * times_block(columns, x, s)
        out[x : x + 1, :] = previous


def sums_kernel(r, z, q, w, local, near, far, cy, back):
    z_a, q_a, w_a = z[...], q[...], w[...]
    p_a = local[...] - cy[...] * (far[...] + near[...])
    lane = lax.broadcasted_iota(jnp.int32, (1, B), 1)
    row = jnp.zeros((1, B), jnp.float32)
    for k, product in enumerate((z_a * r[...], z_a * q_a, w_a * r[...], w_a * q_a, w_a * p_a)):
        total = jnp.sum(jnp.sum(product, axis=0, keepdims=True), axis=1, keepdims=True)
        row = jnp.where(lane == k, total, row)
    rest = jnp.zeros((3, B), jnp.float32)
    for x in range(NW):
        at = slice(x, x + 1)
        tile = jnp.concatenate([z_a[at], q_a[at], w_a[at], p_a[at], row, rest], axis=0)
        for y in range(NY):
            back[y * NW + PLACE[x]] = tile


def share_kernel(back, out):
    part = back[0, 4:5, :]
    for x in range(1, NY * NW):
        part = part + back[x, 4:5, :]
    out[...] = jnp.broadcast_to(part[None], (NZ, 1, B))


def final_kernel(everyone, back, r, solution_out, residual_out):
    total = jnp.sum(everyone[...], axis=0)
    zr, zq, wr, wq, wp = (total[:, k : k + 1] for k in range(5))
    first = zr / zq
    ratio = wq / zq
    second = (first * wq - wr) / (wp - ratio * wq)
    lead = first + second * ratio
    slab = (lax.axis_index("plane_0") + NY - 2) % NY * NW
    for j in range(NW):
        field = back[slab + turned(j)]
        solution_out[0, j : j + 1, :] = lead * field[0:1] - second * field[2:3]
        residual_out[0, j : j + 1, :] = r[j : j + 1] - lead * field[1:2] + second * field[3:4]


def local(kernel, out, name):
    def call(*args):
        specs = tuple(VMEM for _ in out) if isinstance(out, tuple) else VMEM
        args = [pltpu.with_memory_space_constraint(a, pltpu.VMEM) for a in args]
        return pl.pallas_call(
            kernel, out_shape=out, in_specs=[VMEM] * len(args), out_specs=specs, name=name
        )(*args)

    return call


def on_device(right_side, coupling_x, coupling_y, coupling_z, inverse):
    packed, own = pack(inverse, right_side, coupling_z, coupling_x, coupling_y)
    columns = exchanged(packed, WAVE_GROUPS)
    field = on_chip(NW, B)

    def image_part(values):
        return local(image_part_kernel, field, "image_part")(values, faces)

    half = local(first_kernel, field, "first")(columns)
    far, near = neighbours(half)
    parts = (field, field, on_chip(4, NW, B), field)
    base, r, faces, cy = local(settle_first_kernel, parts, "settle_first")(columns, half)
    z = local(backward_kernel, field, "backward")(columns, base, near, far, cy, half)
    far, near = neighbours(z)
    q, half = local(image_kernel, (field, field), "image")(columns, image_part(z), near, far, cy)
    far, near = neighbours(half)
    base = local(settle_kernel, field, "settle")(q, half, faces)
    w = local(backward_kernel, field, "backward")(columns, base, near, far, cy, half)
    far, near = neighbours(w)
    back = local(sums_kernel, on_chip(NY * NW, 8, B), "sums")(r, z, q, w, image_part(w), near, far, cy)
    back = exchanged(back, SLAB_GROUPS)
    share = local(share_kernel, on_chip(NZ, 1, B), "share")(back)
    everyone = exchanged(share, RING_GROUPS)
    out = f32(1, NW, B)
    return local(final_kernel, (out, out), "final")(everyone, back, own)


def solution(mesh):
    torus = Mesh(mesh.devices.reshape(4, 2, 4, 16), ALL)
    return jax.shard_map(
        on_device,
        mesh=torus,
        in_specs=(
            P(WAVE, PLANE, None),
            P(PLANE, None),
            P(WAVE, None),
            P(WAVE, PLANE, None),
            P(WAVE, PLANE, None, None),
        ),
        out_specs=(P(WAVE, PLANE, None), P(WAVE, PLANE, None)),
        check_vma=False,
    )
```

```python
import jax
import jax.numpy as jnp
from jax import lax
from jax.experimental import pallas as pl
from jax.experimental.pallas import tpu as pltpu
from jax.sharding import Mesh
from jax.sharding import PartitionSpec as P

WAVE = ("wave_0", "wave_1")
PLANE = ("plane_0", "plane_1")
ALL = WAVE + PLANE
NW = 8
NP = 64
B = 128
R, CZ, CX, CY = B, B + 1, B + 2, B + 3
ROWS = B + 8

relax = 1.5

VMEM = pl.BlockSpec(memory_space=pltpu.VMEM)
HBM = pl.BlockSpec(memory_space=pl.ANY)


EVEN = (7, 6, 5, 4, 3, 2, 0, 1)
ODD = EVEN[::-1]


def chain_device(position):
    plane, k = divmod(position, NW)
    return (ODD if plane % 2 else EVEN)[k] * NP + plane


def swap_pairs(first):
    pairs = []
    for i in range(first, NW * NP - 1, 2):
        a, b = chain_device(i), chain_device(i + 1)
        pairs += [(a, b), (b, a)]
    return pairs


ORDER = (5, 6, 7, 0, 1, 2, 3, 4)
WAVE_GROUPS = [[w * NP + p for w in ORDER] for p in range(NP)]
PLACE = tuple(ORDER.index(w) for w in range(NW))
NY = 4
NZ = NP // NY
SLAB_GROUPS = [
    [w * NP + (y + 2) % NY * NZ + z for y in range(NY) for w in ORDER] for z in range(NZ)
]
RING_GROUPS = [
    [w * NP + y * NZ + (z + 8) % NZ for z in range(NZ)] for w in range(NW) for y in range(NY)
]
FAR = swap_pairs(1)


def neighbours(values):
    return lax.ppermute(values, ALL, FAR), lax.psum(values, "wave_1")


def exchanged(values, groups):
    return lax.all_to_all(
        values, ALL, split_axis=0, concat_axis=0, tiled=True, axis_index_groups=groups
    )


def f32(*shape):
    return jax.ShapeDtypeStruct(shape, jnp.float32)


def on_chip(*shape):
    return pltpu.VMEM(shape, jnp.float32)


def turned(j):
    parity = lax.axis_index("plane_1") % 2
    even, odd = PLACE[EVEN[j]], PLACE[ODD[j]]
    return even + parity * (odd - even)


def pack_kernel(inverse, right, cz, cx, cy, packed, r_out, cz_v, cx_v, cy_v, sems, small):
    copies = [
        pltpu.make_async_copy(right.at[0], r_out, small.at[0]),
        pltpu.make_async_copy(cz.at[0], cz_v, small.at[1]),
        pltpu.make_async_copy(cx, cx_v, small.at[2]),
        pltpu.make_async_copy(cy, cy_v, small.at[3]),
    ]
    for copy in copies:
        copy.start()
    blocks = [
        pltpu.make_async_copy(inverse.at[0, j], packed.at[turned(j), 0:B, :], sems.at[j])
        for j in range(NW)
    ]
    for copy in blocks:
        copy.start()
    for copy in copies:
        copy.wait()
    r_v, cz_a, cx_a, cy_a = r_out[...], cz_v[...], cx_v[...], cy_v[...]
    for j in range(NW):
        rows = [r_v[j : j + 1], cz_a[j : j + 1], cx_a[j : j + 1], cy_a]
        rows.append(jnp.zeros((ROWS - B - 4, B), jnp.float32))
        packed[turned(j), B:ROWS, :] = jnp.concatenate(rows, axis=0)
    for copy in blocks:
        copy.wait()


def pack(inverse, right_side, coupling_z, coupling_x, coupling_y):
    return pl.pallas_call(
        pack_kernel,
        out_shape=(on_chip(NW, ROWS, B), on_chip(NW, B)),
        in_specs=[HBM] * 5,
        out_specs=(VMEM, VMEM),
        scratch_shapes=[
            pltpu.VMEM((NW, B), jnp.float32),
            pltpu.VMEM((NW, B), jnp.float32),
            pltpu.VMEM((1, B), jnp.float32),
            pltpu.SemaphoreType.DMA((NW,)),
            pltpu.SemaphoreType.DMA((4,)),
        ],
        name="pack",
    )(inverse, right_side, coupling_z, coupling_x, coupling_y)


def times_block(columns, x, vector):
    block = columns[PLACE[x], 0:B, :]
    return jnp.sum(block * vector, axis=1).reshape(1, B)


def forward(columns, source, out):
    cx = columns[0, CX : CX + 1, :]
    previous = None
    for x in range(NW):
        s = source(x)
        if previous is not None:
            s = s + cx * previous
        previous = relax * times_block(columns, x, s)
        out[x : x + 1, :] = previous


def first_kernel(columns, half):
    forward(columns, lambda x: columns[PLACE[x], R : R + 1, :], half)


def image_kernel(columns, local, both, far, cy, own, image, half):
    image[...] = local[...] - cy[...] * (far[...] + (both[...] - own[...]))
    value = image[...]
    forward(columns, lambda x: value[x : x + 1], half)


def column_part(values, centre, cz, upper_z):
    lane = lax.broadcasted_iota(jnp.int32, values.shape, 1)
    below = jnp.where(lane == 0, 0.0, pltpu.roll(values, 1, 1))
    above = jnp.where(lane == B - 1, 0.0, pltpu.roll(values, B - 1, 1))
    return centre * values - cz * below - upper_z * above


def lower(values):
    return jnp.concatenate([jnp.zeros((1, B), jnp.float32), values[:-1]], axis=0)


def upper(values):
    return jnp.concatenate([values[1:], jnp.zeros((1, B), jnp.float32)], axis=0)


def source_part(source, half, cx, cz, upper_z, centre):
    return source - column_part(half, centre, cz, upper_z) + cx * lower(half)


def settle_first_kernel(columns, half, base, r, faces, cy):
    rows = [
        jnp.concatenate([columns[PLACE[x], i : i + 1, :] for x in range(NW)], axis=0)
        for i in (R, CX, CZ, CY)
    ]
    upper_z = pltpu.roll(rows[2], B - 1, 1)
    centre = 2.0 * rows[1] + 2.0 * rows[3] + rows[2] + upper_z
    r[...] = rows[0]
    cy[...] = rows[3]
    for k, face in enumerate((rows[1], rows[2], upper_z, centre)):
        faces[k] = face
    base[...] = source_part(rows[0], half[...], rows[1], rows[2], upper_z, centre)


def settle_kernel(source, half, faces, base):
    base[...] = source_part(source[...], half[...], *(faces[k] for k in range(4)))


def image_part_kernel(values, faces, out):
    v = values[...]
    out[...] = column_part(v, faces[3], faces[1], faces[2]) - faces[0] * (lower(v) + upper(v))


def backward_kernel(columns, base, both, far, cy, half, out):
    source = base[...] + cy[...] * (far[...] + (both[...] - half[...]))
    cx = columns[0, CX : CX + 1, :]
    previous = None
    for x in reversed(range(NW)):
        s = source[x : x + 1]
        if previous is not None:
            s = s + cx * previous
        previous = half[x : x + 1, :] + relax * times_block(columns, x, s)
        out[x : x + 1, :] = previous


def sums_kernel(r, z, q, w, local, both, far, cy, back):
    z_a, q_a, w_a = z[...], q[...], w[...]
    p_a = local[...] - cy[...] * (far[...] + (both[...] - w_a))
    lane = lax.broadcasted_iota(jnp.int32, (1, B), 1)
    row = jnp.zeros((1, B), jnp.float32)
    for k, product in enumerate((z_a * r[...], z_a * q_a, w_a * r[...], w_a * q_a, w_a * p_a)):
        total = jnp.sum(jnp.sum(product, axis=0, keepdims=True), axis=1, keepdims=True)
        row = jnp.where(lane == k, total, row)
    rest = jnp.zeros((3, B), jnp.float32)
    for x in range(NW):
        at = slice(x, x + 1)
        tile = jnp.concatenate([z_a[at], q_a[at], w_a[at], p_a[at], row, rest], axis=0)
        for y in range(NY):
            back[y * NW + PLACE[x]] = tile


def share_kernel(back, out):
    part = back[0, 4:5, :]
    for x in range(1, NY * NW):
        part = part + back[x, 4:5, :]
    out[...] = jnp.broadcast_to(part[None], (NZ, 1, B))


def final_kernel(everyone, back, r, solution_out, residual_out):
    total = jnp.sum(everyone[...], axis=0)
    zr, zq, wr, wq, wp = (total[:, k : k + 1] for k in range(5))
    first = zr / zq
    ratio = wq / zq
    second = (first * wq - wr) / (wp - ratio * wq)
    lead = first + second * ratio
    slab = (lax.axis_index("plane_0") + NY - 2) % NY * NW
    for j in range(NW):
        field = back[slab + turned(j)]
        solution_out[0, j : j + 1, :] = lead * field[0:1] - second * field[2:3]
        residual_out[0, j : j + 1, :] = r[j : j + 1] - lead * field[1:2] + second * field[3:4]


def local(kernel, out, name):
    def call(*args):
        specs = tuple(VMEM for _ in out) if isinstance(out, tuple) else VMEM
        args = [pltpu.with_memory_space_constraint(a, pltpu.VMEM) for a in args]
        return pl.pallas_call(
            kernel, out_shape=out, in_specs=[VMEM] * len(args), out_specs=specs, name=name
        )(*args)

    return call


def on_device(right_side, coupling_x, coupling_y, coupling_z, inverse):
    packed, own = pack(inverse, right_side, coupling_z, coupling_x, coupling_y)
    columns = exchanged(packed, WAVE_GROUPS)
    field = on_chip(NW, B)

    def image_part(values):
        return local(image_part_kernel, field, "image_part")(values, faces)

    half = local(first_kernel, field, "first")(columns)
    far, both = neighbours(half)
    parts = (field, field, on_chip(4, NW, B), field)
    base, r, faces, cy = local(settle_first_kernel, parts, "settle_first")(columns, half)
    z = local(backward_kernel, field, "backward")(columns, base, both, far, cy, half)
    far, both = neighbours(z)
    q, half = local(image_kernel, (field, field), "image")(columns, image_part(z), both, far, cy, z)
    far, both = neighbours(half)
    base = local(settle_kernel, field, "settle")(q, half, faces)
    w = local(backward_kernel, field, "backward")(columns, base, both, far, cy, half)
    far, both = neighbours(w)
    back = local(sums_kernel, on_chip(NY * NW, 8, B), "sums")(r, z, q, w, image_part(w), both, far, cy)
    back = exchanged(back, SLAB_GROUPS)
    share = local(share_kernel, on_chip(NZ, 1, B), "share")(back)
    everyone = exchanged(share, RING_GROUPS)
    out = f32(1, NW, B)
    return local(final_kernel, (out, out), "final")(everyone, back, own)


def solution(mesh):
    torus = Mesh(mesh.devices.reshape(4, 2, 4, 16), ALL)
    return jax.shard_map(
        on_device,
        mesh=torus,
        in_specs=(
            P(WAVE, PLANE, None),
            P(PLANE, None),
            P(WAVE, None),
            P(WAVE, PLANE, None),
            P(WAVE, PLANE, None, None),
        ),
        out_specs=(P(WAVE, PLANE, None), P(WAVE, PLANE, None)),
        check_vma=False,
    )
```

```python
import jax
import jax.numpy as jnp
from jax import lax
from jax.experimental import pallas as pl
from jax.experimental.pallas import tpu as pltpu
from jax.sharding import Mesh
from jax.sharding import PartitionSpec as P

WAVE = ("wave_0", "wave_1")
PLANE = ("plane_0", "plane_1")
ALL = WAVE + PLANE
NW = 8
NP = 64
B = 128
R, CZ, CX, CY = B, B + 1, B + 2, B + 3
ROWS = B + 8

relax = 1.5

VMEM = pl.BlockSpec(memory_space=pltpu.VMEM)
HBM = pl.BlockSpec(memory_space=pl.ANY)


EVEN = (1, 0, 2, 3, 4, 5, 6, 7)
ODD = EVEN[::-1]


def chain_device(position):
    plane, k = divmod(position, NW)
    return (ODD if plane % 2 else EVEN)[k] * NP + plane


def swap_pairs(first):
    pairs = []
    for i in range(first, NW * NP - 1, 2):
        a, b = chain_device(i), chain_device(i + 1)
        pairs += [(a, b), (b, a)]
    return pairs


ORDER = (5, 6, 7, 0, 1, 2, 3, 4)
WAVE_GROUPS = [[w * NP + p for w in ORDER] for p in range(NP)]
PLACE = tuple(ORDER.index(w) for w in range(NW))
NY = 4
NZ = NP // NY
SLAB_GROUPS = [
    [w * NP + (y + 2) % NY * NZ + z for y in range(NY) for w in ORDER] for z in range(NZ)
]
RING_GROUPS = [
    [w * NP + y * NZ + (z + 8) % NZ for z in range(NZ)] for w in range(NW) for y in range(NY)
]
FAR = swap_pairs(1)


def neighbours(values):
    return lax.ppermute(values, ALL, FAR), lax.psum(values, "wave_1")


def exchanged(values, groups):
    return lax.all_to_all(
        values, ALL, split_axis=0, concat_axis=0, tiled=True, axis_index_groups=groups
    )


def f32(*shape):
    return jax.ShapeDtypeStruct(shape, jnp.float32)


def on_chip(*shape):
    return pltpu.VMEM(shape, jnp.float32)


def turned(j):
    parity = lax.axis_index("plane_1") % 2
    even, odd = PLACE[EVEN[j]], PLACE[ODD[j]]
    return even + parity * (odd - even)


def pack_kernel(inverse, right, cz, cx, cy, packed, r_out, cz_v, cx_v, cy_v, sems, small):
    copies = [
        pltpu.make_async_copy(right.at[0], r_out, small.at[0]),
        pltpu.make_async_copy(cz.at[0], cz_v, small.at[1]),
        pltpu.make_async_copy(cx, cx_v, small.at[2]),
        pltpu.make_async_copy(cy, cy_v, small.at[3]),
    ]
    for copy in copies:
        copy.start()
    blocks = [
        pltpu.make_async_copy(inverse.at[0, j], packed.at[turned(j), 0:B, :], sems.at[j])
        for j in range(NW)
    ]
    for copy in blocks:
        copy.start()
    for copy in copies:
        copy.wait()
    r_v, cz_a, cx_a, cy_a = r_out[...], cz_v[...], cx_v[...], cy_v[...]
    for j in range(NW):
        rows = [r_v[j : j + 1], cz_a[j : j + 1], cx_a[j : j + 1], cy_a]
        rows.append(jnp.zeros((ROWS - B - 4, B), jnp.float32))
        packed[turned(j), B:ROWS, :] = jnp.concatenate(rows, axis=0)
    for copy in blocks:
        copy.wait()


def pack(inverse, right_side, coupling_z, coupling_x, coupling_y):
    return pl.pallas_call(
        pack_kernel,
        out_shape=(on_chip(NW, ROWS, B), on_chip(NW, B)),
        in_specs=[HBM] * 5,
        out_specs=(VMEM, VMEM),
        scratch_shapes=[
            pltpu.VMEM((NW, B), jnp.float32),
            pltpu.VMEM((NW, B), jnp.float32),
            pltpu.VMEM((1, B), jnp.float32),
            pltpu.SemaphoreType.DMA((NW,)),
            pltpu.SemaphoreType.DMA((4,)),
        ],
        name="pack",
    )(inverse, right_side, coupling_z, coupling_x, coupling_y)


def times_block(columns, x, vector):
    block = columns[PLACE[x], 0:B, :]
    return jnp.sum(block * vector, axis=1).reshape(1, B)


def forward(columns, source, out):
    cx = columns[0, CX : CX + 1, :]
    previous = None
    for x in range(NW):
        s = source(x)
        if previous is not None:
            s = s + cx * previous
        previous = relax * times_block(columns, x, s)
        out[x : x + 1, :] = previous


def first_kernel(columns, half):
    forward(columns, lambda x: columns[PLACE[x], R : R + 1, :], half)


def image_kernel(columns, local, both, far, cy, own, image, half):
    image[...] = local[...] - cy[...] * (far[...] + (both[...] - own[...]))
    value = image[...]
    forward(columns, lambda x: value[x : x + 1], half)


def column_part(values, centre, cz, upper_z):
    lane = lax.broadcasted_iota(jnp.int32, values.shape, 1)
    below = jnp.where(lane == 0, 0.0, pltpu.roll(values, 1, 1))
    above = jnp.where(lane == B - 1, 0.0, pltpu.roll(values, B - 1, 1))
    return centre * values - cz * below - upper_z * above


def lower(values):
    return jnp.concatenate([jnp.zeros((1, B), jnp.float32), values[:-1]], axis=0)


def upper(values):
    return jnp.concatenate([values[1:], jnp.zeros((1, B), jnp.float32)], axis=0)


def source_part(source, half, cx, cz, upper_z, centre):
    return source - column_part(half, centre, cz, upper_z) + cx * lower(half)


def settle_first_kernel(columns, half, base, r, faces, cy):
    rows = [
        jnp.concatenate([columns[PLACE[x], i : i + 1, :] for x in range(NW)], axis=0)
        for i in (R, CX, CZ, CY)
    ]
    upper_z = pltpu.roll(rows[2], B - 1, 1)
    centre = 2.0 * rows[1] + 2.0 * rows[3] + rows[2] + upper_z
    r[...] = rows[0]
    cy[...] = rows[3]
    for k, face in enumerate((rows[1], rows[2], upper_z, centre)):
        faces[k] = face
    base[...] = source_part(rows[0], half[...], rows[1], rows[2], upper_z, centre)


def settle_kernel(source, half, faces, base):
    base[...] = source_part(source[...], half[...], *(faces[k] for k in range(4)))


def image_part_kernel(values, faces, out):
    v = values[...]
    out[...] = column_part(v, faces[3], faces[1], faces[2]) - faces[0] * (lower(v) + upper(v))


def backward_kernel(columns, base, both, far, cy, half, out):
    source = base[...] + cy[...] * (far[...] + (both[...] - half[...]))
    cx = columns[0, CX : CX + 1, :]
    previous = None
    for x in reversed(range(NW)):
        s = source[x : x + 1]
        if previous is not None:
            s = s + cx * previous
        previous = half[x : x + 1, :] + relax * times_block(columns, x, s)
        out[x : x + 1, :] = previous


def sums_kernel(r, z, q, w, local, both, far, cy, back):
    z_a, q_a, w_a = z[...], q[...], w[...]
    p_a = local[...] - cy[...] * (far[...] + (both[...] - w_a))
    lane = lax.broadcasted_iota(jnp.int32, (1, B), 1)
    row = jnp.zeros((1, B), jnp.float32)
    for k, product in enumerate((z_a * r[...], z_a * q_a, w_a * r[...], w_a * q_a, w_a * p_a)):
        total = jnp.sum(jnp.sum(product, axis=0, keepdims=True), axis=1, keepdims=True)
        row = jnp.where(lane == k, total, row)
    rest = jnp.zeros((3, B), jnp.float32)
    for x in range(NW):
        at = slice(x, x + 1)
        tile = jnp.concatenate([z_a[at], q_a[at], w_a[at], p_a[at], row, rest], axis=0)
        for y in range(NY):
            back[y * NW + PLACE[x]] = tile


def share_kernel(back, out):
    part = back[0, 4:5, :]
    for x in range(1, NY * NW):
        part = part + back[x, 4:5, :]
    out[...] = jnp.broadcast_to(part[None], (NZ, 1, B))


def final_kernel(everyone, back, r, solution_out, residual_out):
    total = jnp.sum(everyone[...], axis=0)
    zr, zq, wr, wq, wp = (total[:, k : k + 1] for k in range(5))
    first = zr / zq
    ratio = wq / zq
    second = (first * wq - wr) / (wp - ratio * wq)
    lead = first + second * ratio
    slab = (lax.axis_index("plane_0") + NY - 2) % NY * NW
    for j in range(NW):
        field = back[slab + turned(j)]
        solution_out[0, j : j + 1, :] = lead * field[0:1] - second * field[2:3]
        residual_out[0, j : j + 1, :] = r[j : j + 1] - lead * field[1:2] + second * field[3:4]


def local(kernel, out, name):
    def call(*args):
        specs = tuple(VMEM for _ in out) if isinstance(out, tuple) else VMEM
        args = [pltpu.with_memory_space_constraint(a, pltpu.VMEM) for a in args]
        return pl.pallas_call(
            kernel, out_shape=out, in_specs=[VMEM] * len(args), out_specs=specs, name=name
        )(*args)

    return call


def on_device(right_side, coupling_x, coupling_y, coupling_z, inverse):
    packed, own = pack(inverse, right_side, coupling_z, coupling_x, coupling_y)
    columns = exchanged(packed, WAVE_GROUPS)
    field = on_chip(NW, B)

    def image_part(values):
        return local(image_part_kernel, field, "image_part")(values, faces)

    half = local(first_kernel, field, "first")(columns)
    far, both = neighbours(half)
    parts = (field, field, on_chip(4, NW, B), field)
    base, r, faces, cy = local(settle_first_kernel, parts, "settle_first")(columns, half)
    z = local(backward_kernel, field, "backward")(columns, base, both, far, cy, half)
    far, both = neighbours(z)
    q, half = local(image_kernel, (field, field), "image")(columns, image_part(z), both, far, cy, z)
    far, both = neighbours(half)
    base = local(settle_kernel, field, "settle")(q, half, faces)
    w = local(backward_kernel, field, "backward")(columns, base, both, far, cy, half)
    far, both = neighbours(w)
    back = local(sums_kernel, on_chip(NY * NW, 8, B), "sums")(r, z, q, w, image_part(w), both, far, cy)
    back = exchanged(back, SLAB_GROUPS)
    share = local(share_kernel, on_chip(NZ, 1, B), "share")(back)
    everyone = exchanged(share, RING_GROUPS)
    out = f32(1, NW, B)
    return local(final_kernel, (out, out), "final")(everyone, back, own)


def solution(mesh):
    torus = Mesh(mesh.devices.reshape(4, 2, 4, 16), ALL)
    return jax.shard_map(
        on_device,
        mesh=torus,
        in_specs=(
            P(WAVE, PLANE, None),
            P(PLANE, None),
            P(WAVE, None),
            P(WAVE, PLANE, None),
            P(WAVE, PLANE, None, None),
        ),
        out_specs=(P(WAVE, PLANE, None), P(WAVE, PLANE, None)),
        check_vma=False,
    )
```

```python
import jax
import jax.numpy as jnp
from jax import lax
from jax.experimental import pallas as pl
from jax.experimental.pallas import tpu as pltpu
from jax.sharding import Mesh
from jax.sharding import PartitionSpec as P

WAVE = ("wave_0", "wave_1")
PLANE = ("plane_0", "plane_1")
ALL = WAVE + PLANE
NW = 8
NP = 64
B = 128
R, CZ, CX, CY = B, B + 1, B + 2, B + 3
ROWS = B + 8

relax = 1.5

VMEM = pl.BlockSpec(memory_space=pltpu.VMEM)
HBM = pl.BlockSpec(memory_space=pl.ANY)


EVEN = (1, 0, 2, 3, 4, 5, 6, 7)
ODD = EVEN[::-1]


def chain_device(position):
    plane, k = divmod(position, NW)
    return (ODD if plane % 2 else EVEN)[k] * NP + plane


def swap_pairs(first):
    pairs = []
    for i in range(first, NW * NP - 1, 2):
        a, b = chain_device(i), chain_device(i + 1)
        pairs += [(a, b), (b, a)]
    return pairs


ORDER = (5, 6, 7, 0, 1, 2, 3, 4)
WAVE_GROUPS = [[w * NP + p for w in ORDER] for p in range(NP)]
PLACE = tuple(ORDER.index(w) for w in range(NW))
NY = 4
NZ = NP // NY
SLAB_GROUPS = [
    [w * NP + (y + 2) % NY * NZ + z for y in range(NY) for w in ORDER] for z in range(NZ)
]
RING_GROUPS = [
    [w * NP + y * NZ + (z + 8) % NZ for z in range(NZ)] for w in range(NW) for y in range(NY)
]
FAR = swap_pairs(1)


def neighbours(values):
    return lax.ppermute(values, ALL, FAR), lax.psum(values, "wave_1")


def exchanged(values, groups):
    return lax.all_to_all(
        values, ALL, split_axis=0, concat_axis=0, tiled=True, axis_index_groups=groups
    )


def f32(*shape):
    return jax.ShapeDtypeStruct(shape, jnp.float32)


def on_chip(*shape):
    return pltpu.VMEM(shape, jnp.float32)


def turned(j):
    parity = lax.axis_index("plane_1") % 2
    even, odd = PLACE[EVEN[j]], PLACE[ODD[j]]
    return even + parity * (odd - even)


def pack_kernel(inverse, right, cz, cx, cy, packed, r_out, cz_v, cx_v, cy_v, sems, small):
    copies = [
        pltpu.make_async_copy(right.at[0], r_out, small.at[0]),
        pltpu.make_async_copy(cz.at[0], cz_v, small.at[1]),
        pltpu.make_async_copy(cx, cx_v, small.at[2]),
        pltpu.make_async_copy(cy, cy_v, small.at[3]),
    ]
    for copy in copies:
        copy.start()
    blocks = [
        pltpu.make_async_copy(inverse.at[0, j], packed.at[turned(j), 0:B, :], sems.at[j])
        for j in range(NW)
    ]
    for copy in blocks:
        copy.start()
    for copy in copies:
        copy.wait()
    r_v, cz_a, cx_a, cy_a = r_out[...], cz_v[...], cx_v[...], cy_v[...]
    for j in range(NW):
        rows = [r_v[j : j + 1], cz_a[j : j + 1], cx_a[j : j + 1], cy_a]
        rows.append(jnp.zeros((ROWS - B - 4, B), jnp.float32))
        packed[turned(j), B:ROWS, :] = jnp.concatenate(rows, axis=0)
    for copy in blocks:
        copy.wait()


def pack(inverse, right_side, coupling_z, coupling_x, coupling_y):
    return pl.pallas_call(
        pack_kernel,
        out_shape=(on_chip(NW, ROWS, B), on_chip(NW, B)),
        in_specs=[HBM] * 5,
        out_specs=(VMEM, VMEM),
        scratch_shapes=[
            pltpu.VMEM((NW, B), jnp.float32),
            pltpu.VMEM((NW, B), jnp.float32),
            pltpu.VMEM((1, B), jnp.float32),
            pltpu.SemaphoreType.DMA((NW,)),
            pltpu.SemaphoreType.DMA((4,)),
        ],
        name="pack",
    )(inverse, right_side, coupling_z, coupling_x, coupling_y)


def times_block(columns, x, vector):
    block = columns[PLACE[x], 0:B, :]
    return jnp.sum(block * vector, axis=1).reshape(1, B)


def forward(columns, source, out):
    cx = relax * columns[0, CX : CX + 1, :]
    previous = None
    for x in range(NW):
        s = relax * source(x)
        if previous is not None:
            s = s + cx * previous
        previous = times_block(columns, x, s)
        out[x : x + 1, :] = previous


def first_kernel(columns, half):
    forward(columns, lambda x: columns[PLACE[x], R : R + 1, :], half)


def image_kernel(columns, local, both, far, cy, own, image, half):
    image[...] = local[...] - cy[...] * (far[...] + (both[...] - own[...]))
    value = image[...]
    forward(columns, lambda x: value[x : x + 1], half)


def column_part(values, centre, cz, upper_z):
    lane = lax.broadcasted_iota(jnp.int32, values.shape, 1)
    below = jnp.where(lane == 0, 0.0, pltpu.roll(values, 1, 1))
    above = jnp.where(lane == B - 1, 0.0, pltpu.roll(values, B - 1, 1))
    return centre * values - cz * below - upper_z * above


def lower(values):
    return jnp.concatenate([jnp.zeros((1, B), jnp.float32), values[:-1]], axis=0)


def upper(values):
    return jnp.concatenate([values[1:], jnp.zeros((1, B), jnp.float32)], axis=0)


def source_part(source, half, cx, cz, upper_z, centre):
    return source - column_part(half, centre, cz, upper_z) + cx * lower(half)


def settle_first_kernel(columns, half, base, r, faces, cy):
    rows = [
        jnp.concatenate([columns[PLACE[x], i : i + 1, :] for x in range(NW)], axis=0)
        for i in (R, CX, CZ, CY)
    ]
    upper_z = pltpu.roll(rows[2], B - 1, 1)
    centre = 2.0 * rows[1] + 2.0 * rows[3] + rows[2] + upper_z
    r[...] = rows[0]
    cy[...] = rows[3]
    for k, face in enumerate((rows[1], rows[2], upper_z, centre)):
        faces[k] = face
    base[...] = source_part(rows[0], half[...], rows[1], rows[2], upper_z, centre)


def settle_kernel(source, half, faces, base):
    base[...] = source_part(source[...], half[...], *(faces[k] for k in range(4)))


def image_part_kernel(values, faces, out):
    v = values[...]
    out[...] = column_part(v, faces[3], faces[1], faces[2]) - faces[0] * (lower(v) + upper(v))


def backward_kernel(columns, base, both, far, cy, half, out):
    source = relax * (base[...] + cy[...] * (far[...] + (both[...] - half[...])))
    cx = relax * columns[0, CX : CX + 1, :]
    previous = None
    for x in reversed(range(NW)):
        s = source[x : x + 1]
        if previous is not None:
            s = s + cx * previous
        previous = half[x : x + 1, :] + times_block(columns, x, s)
        out[x : x + 1, :] = previous


def sums_kernel(r, z, q, w, local, both, far, cy, back):
    z_a, q_a, w_a = z[...], q[...], w[...]
    p_a = local[...] - cy[...] * (far[...] + (both[...] - w_a))
    lane = lax.broadcasted_iota(jnp.int32, (1, B), 1)
    row = jnp.zeros((1, B), jnp.float32)
    for k, product in enumerate((z_a * r[...], z_a * q_a, w_a * r[...], w_a * q_a, w_a * p_a)):
        total = jnp.sum(jnp.sum(product, axis=0, keepdims=True), axis=1, keepdims=True)
        row = jnp.where(lane == k, total, row)
    rest = jnp.zeros((3, B), jnp.float32)
    for x in range(NW):
        at = slice(x, x + 1)
        tile = jnp.concatenate([z_a[at], q_a[at], w_a[at], p_a[at], row, rest], axis=0)
        for y in range(NY):
            back[y * NW + PLACE[x]] = tile


def share_kernel(back, out):
    part = back[0, 4:5, :]
    for x in range(1, NY * NW):
        part = part + back[x, 4:5, :]
    out[...] = jnp.broadcast_to(part[None], (NZ, 1, B))


def final_kernel(everyone, back, r, solution_out, residual_out):
    total = jnp.sum(everyone[...], axis=0)
    zr, zq, wr, wq, wp = (total[:, k : k + 1] for k in range(5))
    first = zr / zq
    ratio = wq / zq
    second = (first * wq - wr) / (wp - ratio * wq)
    lead = first + second * ratio
    slab = (lax.axis_index("plane_0") + NY - 2) % NY * NW
    for j in range(NW):
        field = back[slab + turned(j)]
        solution_out[0, j : j + 1, :] = lead * field[0:1] - second * field[2:3]
        residual_out[0, j : j + 1, :] = r[j : j + 1] - lead * field[1:2] + second * field[3:4]


def local(kernel, out, name):
    def call(*args):
        specs = tuple(VMEM for _ in out) if isinstance(out, tuple) else VMEM
        args = [pltpu.with_memory_space_constraint(a, pltpu.VMEM) for a in args]
        return pl.pallas_call(
            kernel, out_shape=out, in_specs=[VMEM] * len(args), out_specs=specs, name=name
        )(*args)

    return call


def on_device(right_side, coupling_x, coupling_y, coupling_z, inverse):
    packed, own = pack(inverse, right_side, coupling_z, coupling_x, coupling_y)
    columns = exchanged(packed, WAVE_GROUPS)
    field = on_chip(NW, B)

    def image_part(values):
        return local(image_part_kernel, field, "image_part")(values, faces)

    half = local(first_kernel, field, "first")(columns)
    far, both = neighbours(half)
    parts = (field, field, on_chip(4, NW, B), field)
    base, r, faces, cy = local(settle_first_kernel, parts, "settle_first")(columns, half)
    z = local(backward_kernel, field, "backward")(columns, base, both, far, cy, half)
    far, both = neighbours(z)
    q, half = local(image_kernel, (field, field), "image")(columns, image_part(z), both, far, cy, z)
    far, both = neighbours(half)
    base = local(settle_kernel, field, "settle")(q, half, faces)
    w = local(backward_kernel, field, "backward")(columns, base, both, far, cy, half)
    far, both = neighbours(w)
    back = local(sums_kernel, on_chip(NY * NW, 8, B), "sums")(r, z, q, w, image_part(w), both, far, cy)
    back = exchanged(back, SLAB_GROUPS)
    share = local(share_kernel, on_chip(NZ, 1, B), "share")(back)
    everyone = exchanged(share, RING_GROUPS)
    out = f32(1, NW, B)
    return local(final_kernel, (out, out), "final")(everyone, back, own)


def solution(mesh):
    torus = Mesh(mesh.devices.reshape(4, 2, 4, 16), ALL)
    return jax.shard_map(
        on_device,
        mesh=torus,
        in_specs=(
            P(WAVE, PLANE, None),
            P(PLANE, None),
            P(WAVE, None),
            P(WAVE, PLANE, None),
            P(WAVE, PLANE, None, None),
        ),
        out_specs=(P(WAVE, PLANE, None), P(WAVE, PLANE, None)),
        check_vma=False,
    )
```
